128 devices in a mesh: region: 16 (over x, z), sub: 8 (over y, core).
Axes of the slice: x: 4, y: 4, z: 4, core: 2. Of those that a mesh axis runs over, the one named last changes fastest.
Arguments:
- kkt_inverse: bfloat16 [262144, 2048], P(('region', 'sub')), may hold values from -0.125 to 0.125
- cost_terms: bfloat16 [262144, 256], P(('region', 'sub')), may hold values from -6 to 6
- dual_start: float32 [196608, 256], P(('region', 'sub')), may hold values from -4 to 4
- consensus_start: float32 [32768, 256], P(('region', 'sub')), may hold values from -6 to 6
- block_target: int32 [128, 12], P(('region', 'sub')), may hold values from -1 to 31, as said below
Outputs:
- state: float32 [262144, 256], P(('region', 'sub'))
- duals: float32 [196608, 256], P(('region', 'sub'))
- consensus: float32 [32768, 256], P(('region', 'sub'))
- norms: float32 [2, 2], replicated
The draws below stay inside these ranges and needn't reach their ends.
Inputs may be any that keep to these rules, and one draw needn't show every extreme that they name: `block_target`: A device has at most 2 live blocks bound for one region, and every device has exactly 2 for some region. At least 10 of a device's slots are live; some device has all 12 live.
All inputs are finite; a program needn't handle non-finite values.
Results may differ from the reference program's by a relative error of at most 0.0034.
Values sent between devices are 32-bit elements; how exact they have to be, the bound alone decides.
A program may use at most 128 MiB of HBM per device.

```python
import jax
import jax.numpy as jnp
from jax import lax

K = 2048
BLOCK = 128
S = 256
NB = 12
OWNB = 2
CAP = 2
ITERS = 2
N_REGION = 16
N_SUB = 8
DEVICES = 128


def draw_block_target(key, part):
    slots = N_REGION * CAP
    full_device = jax.random.randint(jax.random.fold_in(key, 7), (), 0, DEVICES)

    def one_device(index):
        dkey = jax.random.fold_in(jax.random.fold_in(key, 11), index)
        keys = jax.random.split(dkey, 5)
        first = jax.random.randint(keys[0], (), 0, N_REGION)
        order = jax.random.permutation(keys[1], slots)
        positions = jnp.arange(slots, dtype=jnp.int32)
        peer_of = positions // CAP
        score = jnp.where(peer_of == first, positions % CAP - CAP, order)
        chosen = jnp.argsort(score, stable=True)[:NB]
        peers = (chosen // CAP).astype(jnp.int32)
        active = jax.random.randint(keys[2], (), NB - NB // 6, NB + 1)
        active = jnp.where(index == full_device, NB, active)
        alive = jnp.arange(NB, dtype=jnp.int32) < active
        shuffle = jax.random.permutation(keys[3], NB)
        peers = peers[shuffle]
        alive = alive[shuffle]
        owned_index = jax.random.randint(keys[4], (NB,), 0, OWNB)
        return jnp.where(alive, peers * OWNB + owned_index, -1).astype(jnp.int32)
    return jax.vmap(one_device)(jnp.arange(DEVICES, dtype=jnp.int32))


def block_levels(stream_key, dims, shards, low, high):
    gain = 1.0
    for axis_at, shards_of in shards:
        steps = jax.random.uniform(jax.random.fold_in(jax.random.fold_in(stream_key, 6), axis_at), (shards_of,), jnp.float32, low / len(shards), high / len(shards))
        gain = gain * jnp.repeat(jnp.exp(steps), dims[axis_at] // shards_of).reshape((-1,) + (1,) * (len(dims) - 1 - axis_at))
    return gain


def bell_draw(rng, shape, width, reach, pieces=(), kind=jnp.bfloat16):
    values = width * jax.random.normal(rng, shape, jnp.float32)
    if pieces:
        values = values * block_levels(rng, shape, pieces, -0.22, 0.18)
    return jnp.clip(values, -reach, reach).astype(kind)


def setup_inputs(seed: int = 0) -> dict:
    arg_keys = jax.random.split(jax.random.key(seed), 6)
    return {
        "kkt_inverse": bell_draw(arg_keys[0], (DEVICES * K, K), K ** -0.5, 0.125, ((0, 128),)),
        "cost_terms": bell_draw(arg_keys[1], (DEVICES * K, S), 1.0, 6.0, ((0, 128),)),
        "dual_start": bell_draw(arg_keys[2], (DEVICES * NB * BLOCK, S), 0.5, 4.0, ((0, 128),), jnp.float32),
        "consensus_start": bell_draw(arg_keys[3], (DEVICES * OWNB * BLOCK, S), 1.0, 6.0, ((0, 128),), jnp.float32),
        "block_target": draw_block_target(jax.random.fold_in(arg_keys[5], 71), 0),
    }


penalty = 1.5

def reference(kkt_inverse, cost_terms, dual_start, consensus_start, block_target):
    highest = lax.Precision.HIGHEST
    bound_rows = NB * BLOCK
    inverse = kkt_inverse.reshape(DEVICES, K, K)
    cost = cost_terms.reshape(DEVICES, K, S)
    base = lax.map(lambda pair: jnp.dot(pair[0], pair[1], preferred_element_type=jnp.float32), (inverse, cost))
    device = jnp.arange(DEVICES, dtype=jnp.int32)
    sub_index = device % N_SUB
    live = block_target >= 0
    livef = live.astype(jnp.float32)
    owner = block_target // OWNB * N_SUB + sub_index[:, None]
    slot = jnp.where(live, owner * OWNB + block_target % OWNB, -1)
    onehot = (slot[:, :, None] == jnp.arange(DEVICES * OWNB, dtype=jnp.int32)[None, None, :]).astype(jnp.float32)
    counts = lax.optimization_barrier(jnp.sum(onehot, axis=(0, 1)))
    floor_counts = jnp.maximum(counts, 1.0)
    dual = dual_start.reshape(DEVICES, NB, BLOCK * S)
    cons = consensus_start.reshape(DEVICES * OWNB, BLOCK * S)

    def fetch(values):
        return jnp.einsum('dng,gm->dnm', onehot, values, precision=highest)

    def couple(pair):
        return jnp.dot(pair[0][:, :bound_rows], pair[1], preferred_element_type=jnp.float32)
    fetched = fetch(cons)
    rows = []
    field = base
    for step in range(ITERS):
        drive = (penalty * livef[:, :, None] * (fetched - dual)).reshape(DEVICES, bound_rows, S).astype(jnp.bfloat16)
        field = base + lax.map(couple, (inverse, drive))
        copies = field[:, :bound_rows].reshape(DEVICES, NB, BLOCK * S)
        sums = jnp.einsum('dng,dnm->gm', onehot, copies + dual, precision=highest)
        renewed = sums / floor_counts[:, None]
        fetched = fetch(renewed)
        gap = copies - fetched
        primal = jnp.sum(livef[:, :, None] * gap * gap)
        change = renewed - cons
        moved = penalty * penalty * jnp.sum(counts[:, None] * change * change)
        dual = dual + livef[:, :, None] * gap
        cons = renewed
        rows.append(jnp.stack([primal, moved]))
    table = jnp.stack(rows)
    norms = jnp.sqrt(table / (DEVICES * S * BLOCK))
    state = field.reshape(DEVICES * K, S)
    return (state, dual.reshape(DEVICES * NB * BLOCK, S), cons.reshape(DEVICES * OWNB * BLOCK, S), norms)
```

```python
import functools

import jax
import jax.numpy as jnp
from jax import lax
from jax.experimental import pallas as pl
from jax.experimental.pallas import tpu as pltpu
from jax.sharding import PartitionSpec as P

MESH = pl.DeviceIdType.MESH
BLOCK = 128
ITERS = 2
RING = 4
ROWS = 16
LANES = 128
penalty = 1.5


def ring_add(a, e):
    return lax.rem(a + e, RING)


def kernel(
    kkt_ref, cost_ref, dual_ref, cons_ref, target_ref,
    state_ref, duals_ref, consensus_ref, norms_ref,
    kkt, cost, base, state, dual, cons, drive, tables, table_s, count_v, count_s, part, totals_a, totals_b,
    *rest,
):
    nb = target_ref.shape[1]
    owned = cons_ref.shape[0]
    n_region = RING * RING
    n_sub = lax.axis_size("sub")
    n_pos = n_region * owned
    mine = RING * owned
    bound = nb * BLOCK
    order = rest[0].shape[0]
    streams = [(c, h) for c in range(2) for h in range(2)]
    bufs = {}
    names = ("send", "got", "psum", "got2", "grid", "back", "fetched", "own")
    rest = list(rest)
    for s in streams:
        for name in names:
            bufs[name, s] = rest.pop(0)
    sem_local, sem_table, sem_init, sem_v, sem_p, sem_q, sem_w, sem_o, sem_n = rest
    del order

    r = lax.axis_index("region")
    sub = lax.axis_index("sub")
    x = r // RING
    z = lax.rem(r, RING)

    def first(h, e):
        return ring_add(x, e) * RING + z if h == 0 else x * RING + ring_add(z, e)

    def second(h, e):
        return first(1 - h, e)

    c1 = (x, z)
    c2 = (z, x)

    def remote(src, dst, sems, index, region):
        return pltpu.make_async_remote_copy(
            src_ref=src, dst_ref=dst, send_sem=sems.at[(0, *index)], recv_sem=sems.at[(1, *index)],
            device_id={"region": region}, device_id_type=MESH,
        )

    local = [
        pltpu.make_async_copy(cons_ref, cons, sem_local.at[0]),
        pltpu.make_async_copy(cost_ref, cost, sem_local.at[1]),
        pltpu.make_async_copy(dual_ref, dual, sem_local.at[2]),
        pltpu.make_async_copy(kkt_ref, kkt, sem_local.at[3]),
    ]
    for copy in local:
        copy.start()

    barrier = pltpu.get_barrier_semaphore()
    for e in range(1, n_region):
        pl.semaphore_signal(
            barrier, inc=1, device_id={"region": lax.rem(r + e, n_region)}, device_id_type=MESH
        )
    for e in range(1, n_sub):
        pl.semaphore_signal(barrier, inc=1, device_id={"sub": lax.rem(sub + e, n_sub)}, device_id_type=MESH)

    lane = lax.broadcasted_iota(jnp.int32, (8, LANES), 1)
    row = lax.broadcasted_iota(jnp.int32, (8, LANES), 0)
    none = jnp.full((8, LANES), nb, jnp.int32)
    one_a, one_b, two_a, two_b = none, none, none, none
    places = jnp.full((8, LANES), n_pos, jnp.int32)
    for s in range(nb):
        t = target_ref[0, s]
        pos_b = t
        pos_a = lax.rem(t // owned, RING) * mine + (t // (owned * RING)) * owned + lax.rem(t, owned)
        pos_a = jnp.where(t >= 0, pos_a, -1)
        hit_a = lane == pos_a
        hit_b = lane == pos_b
        two_a = jnp.where(hit_a & (one_a < nb), s, two_a)
        one_a = jnp.where(hit_a & (one_a == nb), s, one_a)
        two_b = jnp.where(hit_b & (one_b < nb), s, two_b)
        one_b = jnp.where(hit_b & (one_b == nb), s, one_b)
        here = jnp.where(row == 4, pos_a, pos_b)
        places = jnp.where((lane == s) & (t >= 0), here, places)
    tile = jnp.where(row == 0, one_a, places)
    tile = jnp.where(row == 1, two_a, tile)
    tile = jnp.where(row == 2, one_b, tile)
    tile = jnp.where(row == 3, two_b, tile)
    tables[pl.ds(r, 1)] = tile[None]

    zero = jnp.zeros((ROWS, LANES), jnp.float32)
    for s in streams:
        for p in range(RING):
            bufs["send", s][p, nb] = zero
        for p in range(RING - 1):
            bufs["got", s][p, nb] = zero
        bufs["grid", s][n_pos] = zero

    local[0].wait()
    pl.semaphore_wait(barrier, n_region - 1 + n_sub - 1)

    init = {}
    for s in streams:
        c, h = s
        for e in range(1, RING):
            p = ring_add(c1[h], e)
            at = pl.multiple_of(c2[h] * mine + c1[h] * owned, owned)
            src = cons.at[:, pl.ds(pl.multiple_of(h * RING * ROWS + p * ROWS, ROWS), ROWS), pl.ds(c * LANES, LANES)]
            init[s, e] = remote(src, bufs["grid", s].at[pl.ds(at, owned)], sem_init, (c, h, e - 1), first(h, e))
            init[s, e].start()
    table_copies = []
    for e in range(1, n_region):
        copy = remote(tables.at[r], tables.at[r], sem_table, (e - 1,), lax.rem(r + e, n_region))
        copy.start()
        table_copies.append(copy)
    for s in streams:
        c, h = s
        for o in range(owned):
            rows = pl.ds(pl.multiple_of(h * RING * ROWS + c1[h] * ROWS, ROWS), ROWS)
            bufs["grid", s][c2[h] * mine + c1[h] * owned + o] = cons[o, rows, c * LANES : (c + 1) * LANES]

    def send_grid(s):
        c, h = s
        copies = []
        at = pl.ds(pl.multiple_of(c2[h] * mine, mine), mine)
        for e in range(1, RING):
            copy = remote(
                bufs["grid", s].at[at], bufs["grid", s].at[at], sem_q, (c, h, e - 1), second(h, e)
            )
            copy.start()
            copies.append(copy)
        return copies

    q_copies, w_copies, v_copies, p_copies = {}, {}, {}, {}
    for s in streams:
        for e in range(1, RING):
            init[s, e].wait()
        q_copies[s] = send_grid(s)

    for copy in table_copies:
        copy.wait()
    peers = [r] + [first(0, e) for e in range(1, RING)] + [first(1, e) for e in range(1, RING)]
    moves = [
        pltpu.make_async_copy(tables.at[peer], table_s.at[i], sem_local.at[4 + i]) for i, peer in enumerate(peers)
    ]
    for move in moves:
        move.start()
    every = tables[...]
    used = jnp.sum((every < nb).astype(jnp.int32), axis=0).astype(jnp.float32)
    count_a = used[0:1] + used[1:2]
    count_b = used[2:3] + used[3:4]
    count_v[...] = jnp.where(row == 0, count_a, count_b)
    counting = pltpu.make_async_copy(count_v, count_s, sem_local.at[11])
    counting.start()
    for move in moves:
        move.wait()
    counting.wait()

    def table_of(h, e):
        return 0 if e == 0 else (e if h == 0 else RING - 1 + e)

    def live(s):
        return jnp.where(target_ref[0, s] >= 0, 1.0, 0.0).astype(jnp.float32)

    local[1].wait()
    local[3].wait()

    half = 256

    def base_rows(i, _):
        at = pl.ds(pl.multiple_of(i * half, half), half)
        base[at] = jnp.dot(kkt[at], cost[...], preferred_element_type=jnp.float32)
        return 0

    lax.fori_loop(0, kkt.shape[0] // half, base_rows, 0)
    local[2].wait()

    def gather_send(s, before):
        c, h = s
        for copy in q_copies[s]:
            copy.wait_recv()
        for copy in before:
            copy.wait_send()
        copies = []
        grid = bufs["grid", s]
        for e in (1, 3, 2, 0):
            t = table_of(h, e)

            def one(slot, _):
                value = grid[table_s[t, 4 + h, slot]]
                if e:
                    bufs["back", s][e - 1, slot] = value
                else:
                    bufs["own", s][slot] = value
                return 0

            lax.fori_loop(0, nb, one, 0, unroll=4)
            if e:
                copy = remote(
                    bufs["back", s].at[e - 1], bufs["fetched", s].at[e - 1], sem_w, (c, h, e - 1), first(h, e)
                )
                copy.start()
                copies.append(copy)
        return copies

    def fetched_rows(s, slot, p):
        c, h = s
        return bufs["fetched", s][lax.rem(c1[h] - p + RING, RING), slot]

    def own_into_place(s):
        pass

    part_primal = {}

    def update(c, step):
        cols = pl.ds(c * LANES, LANES)

        def one(slot, total):
            alive = live(slot)
            for h in range(2):
                s = (c, h)
                for e in range(RING):
                    p = lax.rem(c1[h] - e + RING, RING)
                    value = bufs["own", s][slot] if e == 0 else bufs["fetched", s][e - 1, slot]
                    in_block = pl.ds(pl.multiple_of(h * RING * ROWS + p * ROWS, ROWS), ROWS)
                    old = dual[slot, in_block, cols]
                    at = pl.ds(pl.multiple_of(slot * BLOCK + h * RING * ROWS + p * ROWS, ROWS), ROWS)
                    if step > 0:
                        gap = state[at, cols] - value
                        total = total + alive * gap * gap
                        old = old + alive * gap
                        dual[slot, in_block, cols] = old
                    if step < ITERS:
                        drive[at, cols] = (penalty * alive * (value - old)).astype(jnp.bfloat16)
            return total

        return lax.fori_loop(0, nb, one, jnp.zeros((ROWS, LANES), jnp.float32))

    slots_at_once = 4
    chunk = slots_at_once * BLOCK

    def couple_send(c, step):
        cols = pl.ds(c * LANES, LANES)
        for h in range(2):
            for copy in v_copies.get((c, h), ()):
                copy.wait_send()

        def one(i, _):
            at = pl.ds(pl.multiple_of(i * chunk, chunk), chunk)
            rows = base[at, cols] + jnp.dot(
                kkt[at, 0:bound], drive[:, cols], preferred_element_type=jnp.float32
            )
            state[at, cols] = rows
            for j in range(slots_at_once):
                slot = i * slots_at_once + j
                v = rows[j * BLOCK : (j + 1) * BLOCK] + dual[slot, :, cols]
                for h in range(2):
                    for p in range(RING):
                        lo = h * RING * ROWS + p * ROWS
                        bufs["send", (c, h)][p, slot] = v[lo : lo + ROWS]
            return 0

        lax.fori_loop(0, nb // slots_at_once, one, 0)
        for h in range(2):
            s = (c, h)
            copies = []
            for e in (1, 3, 2):
                p = ring_add(c1[h], e)
                copy = remote(
                    bufs["send", s].at[p, pl.ds(0, nb)], bufs["got", s].at[e - 1, pl.ds(0, nb)],
                    sem_v, (c, h, e - 1), first(h, e),
                )
                copy.start()
                copies.append(copy)
            v_copies[s] = copies

    def reduce_send(s):
        c, h = s
        for copy in v_copies[s]:
            copy.wait_recv()
        for copy in p_copies.get(s, ()):
            copy.wait_send()
        mine_at = c1[h]

        def one(pos, _):
            t = table_of(h, 0)
            value = bufs["send", s][mine_at, table_s[t, 2 * h, pos]] + bufs["send", s][mine_at, table_s[t, 2 * h + 1, pos]]
            for e in range(1, RING):
                t = table_of(h, RING - e)
                value = value + bufs["got", s][e - 1, table_s[t, 2 * h, pos]]
                value = value + bufs["got", s][e - 1, table_s[t, 2 * h + 1, pos]]
            bufs["psum", s][pos] = value
            return 0

        lax.fori_loop(0, n_pos, one, 0, unroll=4)
        copies = []
        for e in (1, 3, 2):
            p = ring_add(c2[h], e)
            copy = remote(
                bufs["psum", s].at[pl.ds(pl.multiple_of(p * mine, mine), mine)], bufs["got2", s].at[e - 1],
                sem_p, (c, h, e - 1), second(h, e),
            )
            copy.start()
            copies.append(copy)
        p_copies[s] = copies

    def renew_send(s, moved):
        c, h = s
        for copy in p_copies[s]:
            copy.wait_recv()
        for copy in q_copies[s]:
            copy.wait_send()
        for k in range(mine):
            at = c2[h] * mine + k
            total = bufs["psum", s][at]
            for e in range(1, RING):
                total = total + bufs["got2", s][e - 1, k]
            count = count_s[h, at]
            new = total / jnp.maximum(count, 1.0)
            change = new - bufs["grid", s][at]
            moved = moved + count * (change * change)
            bufs["grid", s][at] = new
        q_copies[s] = send_grid(s)
        return moved

    for s in streams:
        w_copies[s] = gather_send(s, ())
    sums = []
    owner_copies = []
    for step in range(ITERS):
        for c in range(2):
            for h in range(2):
                for copy in w_copies[c, h]:
                    copy.wait_recv()
            primal = update(c, step)
            if step > 0:
                sums[2 * (step - 1)] = sums[2 * (step - 1)] + primal
            couple_send(c, step)
        if step == ITERS - 1:
            tail = pl.ds(bound, kkt.shape[0] - bound)
            state[tail] = base[tail] + jnp.dot(
                kkt[tail, 0:bound], drive[...], preferred_element_type=jnp.float32
            )
            state_out = pltpu.make_async_copy(state, state_ref, sem_local.at[12])
            state_out.start()
        for s in streams:
            reduce_send(s)
        moved = zero
        for s in streams:
            moved = renew_send(s, moved)
            if step == ITERS - 1:
                c, h = s
                for e in range(1, RING):
                    p = ring_add(c1[h], e)
                    at = pl.multiple_of(c2[h] * mine + p * owned, owned)
                    rows = pl.ds(pl.multiple_of(h * RING * ROWS + c1[h] * ROWS, ROWS), ROWS)
                    copy = remote(
                        bufs["grid", s].at[pl.ds(at, owned)], cons.at[:, rows, pl.ds(c * LANES, LANES)],
                        sem_o, (c, h, e - 1), first(h, e),
                    )
                    copy.start()
                    owner_copies.append(copy)
                rows = pl.ds(pl.multiple_of(h * RING * ROWS + c1[h] * ROWS, ROWS), ROWS)
                for o in range(owned):
                    cons[o, rows, c * LANES : (c + 1) * LANES] = bufs["grid", s][c2[h] * mine + c1[h] * owned + o]
        sums.append(zero)
        sums.append((penalty * penalty) * moved)
        for s in streams:
            w_copies[s] = gather_send(s, w_copies[s])
    for c in range(2):
        for h in range(2):
            for copy in w_copies[c, h]:
                copy.wait_recv()
        sums[2 * (ITERS - 1)] = sums[2 * (ITERS - 1)] + update(c, ITERS)
    dual_out = pltpu.make_async_copy(dual, duals_ref, sem_local.at[13])
    dual_out.start()

    tile = jnp.zeros((8, LANES), jnp.float32)
    for q, value in enumerate(sums):
        tile = jnp.where(row == q, jnp.sum(value, axis=0, keepdims=True), tile)
    totals_a[pl.ds(r, 1)] = tile[None]
    copies = []
    for e in range(1, n_region):
        copy = remote(totals_a.at[r], totals_a.at[r], sem_n, (e - 1,), lax.rem(r + e, n_region))
        copy.start()
        copies.append(copy)
    for copy in owner_copies:
        copy.wait()
    cons_out = pltpu.make_async_copy(cons, consensus_ref, sem_local.at[14])
    cons_out.start()
    for copy in copies:
        copy.wait()
    totals_b[pl.ds(sub, 1)] = jnp.sum(totals_a[...], axis=0, keepdims=True)
    copies = []
    for e in range(1, n_sub):
        copy = pltpu.make_async_remote_copy(
            src_ref=totals_b.at[sub], dst_ref=totals_b.at[sub],
            send_sem=sem_n.at[0, n_region - 2 + e], recv_sem=sem_n.at[1, n_region - 2 + e],
            device_id={"sub": lax.rem(sub + e, n_sub)}, device_id_type=MESH,
        )
        copy.start()
        copies.append(copy)
    for copy in copies:
        copy.wait()
    table = jnp.sum(jnp.sum(totals_b[...], axis=0), axis=1, keepdims=True)
    scale = 1.0 / (n_region * n_sub * 2 * LANES * BLOCK)
    norms_ref[...] = jnp.broadcast_to(jnp.sqrt(table * scale), (8, LANES))

    for s in streams:
        for copy in v_copies[s] + p_copies[s] + q_copies[s] + w_copies[s]:
            copy.wait_send()
    state_out.wait()
    dual_out.wait()
    cons_out.wait()


def shards(kkt_inverse, cost_terms, dual_start, consensus_start, block_target):
    order, scen = cost_terms.shape
    nb = block_target.shape[1]
    owned = consensus_start.shape[0] // BLOCK
    n_region = RING * RING
    n_sub = lax.axis_size("sub")
    n_pos = n_region * owned
    mine = RING * owned
    f32 = jnp.float32
    dma = pltpu.SemaphoreType.DMA
    per_stream = [
        pltpu.VMEM((RING, nb + 1, ROWS, LANES), f32),
        pltpu.VMEM((RING - 1, nb + 1, ROWS, LANES), f32),
        pltpu.VMEM((n_pos, ROWS, LANES), f32),
        pltpu.VMEM((RING - 1, mine, ROWS, LANES), f32),
        pltpu.VMEM((n_pos + 1, ROWS, LANES), f32),
        pltpu.VMEM((RING - 1, nb, ROWS, LANES), f32),
        pltpu.VMEM((RING - 1, nb, ROWS, LANES), f32),
        pltpu.VMEM((nb, ROWS, LANES), f32),
    ]
    state, duals, consensus, norms = pl.pallas_call(
        kernel,
        out_shape=(
            jax.ShapeDtypeStruct((order, scen), f32),
            jax.ShapeDtypeStruct((nb, BLOCK, scen), f32),
            jax.ShapeDtypeStruct((owned, BLOCK, scen), f32),
            jax.ShapeDtypeStruct((8, LANES), f32),
        ),
        in_specs=[pl.BlockSpec(memory_space=pl.ANY)] * 4 + [pl.BlockSpec(memory_space=pltpu.SMEM)],
        out_specs=(pl.BlockSpec(memory_space=pl.ANY),) * 3 + (pl.BlockSpec(memory_space=pltpu.VMEM),),
        scratch_shapes=[
            pltpu.VMEM((order, order), jnp.bfloat16),
            pltpu.VMEM((order, scen), jnp.bfloat16),
            pltpu.VMEM((order, scen), f32),
            pltpu.VMEM((order, scen), f32),
            pltpu.VMEM((nb, BLOCK, scen), f32),
            pltpu.VMEM((owned, BLOCK, scen), f32),
            pltpu.VMEM((nb * BLOCK, scen), jnp.bfloat16),
            pltpu.VMEM((n_region, 8, LANES), jnp.int32),
            pltpu.SMEM((2 * RING - 1, 8, LANES), jnp.int32),
            pltpu.VMEM((8, LANES), f32),
            pltpu.SMEM((8, LANES), f32),
            pltpu.VMEM((8, LANES), f32),
            pltpu.VMEM((n_region, 8, LANES), f32),
            pltpu.VMEM((n_sub, 8, LANES), f32),
        ]
        + per_stream * 4
        + [
            dma((15,)),
            dma((2, n_region - 1)),
            dma((2, 2, 2, RING - 1)),
            dma((2, 2, 2, RING - 1)),
            dma((2, 2, 2, RING - 1)),
            dma((2, 2, 2, RING - 1)),
            dma((2, 2, 2, RING - 1)),
            dma((2, 2, 2, RING - 1)),
            dma((2, n_region - 1 + n_sub - 1)),
        ],
        compiler_params=pltpu.CompilerParams(
            collective_id=0, has_side_effects=True, vmem_limit_bytes=60 * 2**20
        ),
        name="admm",
    )(
        kkt_inverse,
        cost_terms,
        dual_start.reshape(nb, BLOCK, scen),
        consensus_start.reshape(owned, BLOCK, scen),
        block_target,
    )
    return (
        state,
        duals.reshape(nb * BLOCK, scen),
        consensus.reshape(owned * BLOCK, scen),
        norms[: 2 * ITERS, 0].reshape(ITERS, 2),
    )


def solution(mesh):
    both = P(("region", "sub"), None)
    return jax.shard_map(
        shards, mesh=mesh, in_specs=(both,) * 5, out_specs=(both, both, both, P()), check_vma=False
    )
```

```python
import functools

import jax
import jax.numpy as jnp
from jax import lax
from jax.experimental import pallas as pl
from jax.experimental.pallas import tpu as pltpu
from jax.sharding import PartitionSpec as P

MESH = pl.DeviceIdType.MESH
BLOCK = 128
ITERS = 2
RING = 4
ROWS = 16
LANES = 128
penalty = 1.5


def ring_add(a, e):
    return lax.rem(a + e, RING)


def kernel(
    kkt_ref, cost_ref, dual_ref, cons_ref, target_ref,
    state, dual, consensus, norms_ref,
    kkt, cost, base, cons, drive, tables, table_s, partial_v, count_v, count_s, totals_a, totals_b,
    *rest,
):
    nb = target_ref.shape[1]
    owned = cons_ref.shape[0]
    n_region = RING * RING
    n_sub = lax.axis_size("sub")
    n_pos = n_region * owned
    mine = RING * owned
    bound = nb * BLOCK
    streams = [(c, h) for c in range(2) for h in range(2)]
    bufs = {}
    names = ("send", "got", "psum", "got2", "grid", "back", "fetched", "own", "held")
    rest = list(rest)
    for s in streams:
        for name in names:
            bufs[name, s] = rest.pop(0)
    sem_local, sem_table, sem_count, sem_init, sem_v, sem_p, sem_q, sem_w, sem_o, sem_n = rest

    r = lax.axis_index("region")
    sub = lax.axis_index("sub")
    x = r // RING
    z = lax.rem(r, RING)

    def first(h, e):
        return ring_add(x, e) * RING + z if h == 0 else x * RING + ring_add(z, e)

    def second(h, e):
        return first(1 - h, e)

    c1 = (x, z)
    c2 = (z, x)

    def remote(src, dst, sems, index, region):
        return pltpu.make_async_remote_copy(
            src_ref=src, dst_ref=dst, send_sem=sems.at[(0, *index)], recv_sem=sems.at[(1, *index)],
            device_id={"region": region}, device_id_type=MESH,
        )

    local = [
        pltpu.make_async_copy(cons_ref, cons, sem_local.at[0]),
        pltpu.make_async_copy(cost_ref, cost, sem_local.at[1]),
        pltpu.make_async_copy(dual_ref, dual, sem_local.at[2]),
        pltpu.make_async_copy(kkt_ref, kkt, sem_local.at[3]),
    ]
    for copy in local:
        copy.start()

    barrier = pltpu.get_barrier_semaphore()
    near = [(h, e) for h in range(2) for e in range(1, RING)]
    for h, e in near:
        pl.semaphore_signal(barrier, inc=1, device_id={"region": first(h, e)}, device_id_type=MESH)
    for e in range(1, n_sub):
        pl.semaphore_signal(barrier, inc=1, device_id={"sub": lax.rem(sub + e, n_sub)}, device_id_type=MESH)

    lane = lax.broadcasted_iota(jnp.int32, (8, LANES), 1)
    row = lax.broadcasted_iota(jnp.int32, (8, LANES), 0)
    none = jnp.full((8, LANES), nb, jnp.int32)
    one_a, one_b, two_a, two_b = none, none, none, none
    places = jnp.full((8, LANES), n_pos, jnp.int32)
    for s in range(nb):
        t = target_ref[0, s]
        pos_b = t
        pos_a = lax.rem(t // owned, RING) * mine + (t // (owned * RING)) * owned + lax.rem(t, owned)
        pos_a = jnp.where(t >= 0, pos_a, -1)
        hit_a = lane == pos_a
        hit_b = lane == pos_b
        two_a = jnp.where(hit_a & (one_a < nb), s, two_a)
        one_a = jnp.where(hit_a & (one_a == nb), s, one_a)
        two_b = jnp.where(hit_b & (one_b < nb), s, two_b)
        one_b = jnp.where(hit_b & (one_b == nb), s, one_b)
        here = jnp.where(row == 4, pos_a, pos_b)
        places = jnp.where((lane == s) & (t >= 0), here, places)
    tile = jnp.where(row == 0, one_a, places)
    tile = jnp.where(row == 1, two_a, tile)
    tile = jnp.where(row == 2, one_b, tile)
    tile = jnp.where(row == 3, two_b, tile)
    tables[0] = tile

    zero = jnp.zeros((ROWS, LANES), jnp.float32)
    for s in streams:
        for p in range(RING):
            bufs["send", s][p, nb] = zero
        for p in range(RING - 1):
            bufs["got", s][p, nb] = zero
        bufs["grid", s][n_pos] = zero

    local[0].wait()
    pl.semaphore_wait(barrier, len(near) + n_sub - 1)

    init = {}
    for s in streams:
        c, h = s
        for e in range(1, RING):
            p = ring_add(c1[h], e)
            at = pl.multiple_of(c2[h] * mine + c1[h] * owned, owned)
            src = cons.at[:, pl.ds(pl.multiple_of(h * RING * ROWS + p * ROWS, ROWS), ROWS), pl.ds(c * LANES, LANES)]
            init[s, e] = remote(src, bufs["grid", s].at[pl.ds(at, owned)], sem_init, (c, h, e - 1), first(h, e))
            init[s, e].start()
    table_copies = []
    for h, e in near:
        i = (RING - 1) * h + e
        copy = remote(tables.at[0], tables.at[i], sem_table, (i,), first(h, e))
        copy.start()
        table_copies.append(copy)
    for s in streams:
        c, h = s
        for o in range(owned):
            rows = pl.ds(pl.multiple_of(h * RING * ROWS + c1[h] * ROWS, ROWS), ROWS)
            bufs["grid", s][c2[h] * mine + c1[h] * owned + o] = cons[o, rows, c * LANES : (c + 1) * LANES]

    def send_grid(s):
        c, h = s
        copies = []
        at = pl.ds(pl.multiple_of(c2[h] * mine, mine), mine)
        for e in range(1, RING):
            copy = remote(
                bufs["grid", s].at[at], bufs["grid", s].at[at], sem_q, (c, h, e - 1), second(h, e)
            )
            copy.start()
            copies.append(copy)
        return copies

    q_copies, w_copies, v_copies, p_copies = {}, {}, {}, {}
    for s in streams:
        for e in range(1, RING):
            init[s, e].wait()
        q_copies[s] = send_grid(s)

    for copy in table_copies:
        copy.wait()
    to_scalar = pltpu.make_async_copy(tables, table_s, sem_local.at[4])
    to_scalar.start()

    def uses(i, h):
        hits = (tables[i] < nb).astype(jnp.float32)
        return hits[2 * h : 2 * h + 1] + hits[2 * h + 1 : 2 * h + 2]

    over = []
    for h in range(2):
        total = uses(0, h)
        for e in range(1, RING):
            total = total + uses((RING - 1) * h + e, h)
        over.append(total)
    partial_v[0] = jnp.where(row == 0, over[0], over[1])
    count_copies = []
    for h, e in near:
        i = (RING - 1) * h + e
        copy = remote(partial_v.at[0], partial_v.at[i], sem_count, (i,), first(h, e))
        copy.start()
        count_copies.append(copy)
    to_scalar.wait()

    def table_of(h, e):
        return 0 if e == 0 else (RING - 1) * h + e

    def live(s):
        return jnp.where(target_ref[0, s] >= 0, 1.0, 0.0).astype(jnp.float32)

    local[1].wait()
    local[3].wait()

    half = 256

    def base_rows(i, _):
        at = pl.ds(pl.multiple_of(i * half, half), half)
        base[at] = jnp.dot(kkt[at], cost[...], preferred_element_type=jnp.float32)
        return 0

    lax.fori_loop(0, kkt.shape[0] // half, base_rows, 0)
    local[2].wait()

    for copy in count_copies:
        copy.wait()
    count_a = partial_v[0, 0:1] + partial_v[RING, 0:1]
    count_b = partial_v[0, 1:2] + partial_v[1, 1:2]
    for e in range(2, RING):
        count_a = count_a + partial_v[RING - 1 + e, 0:1]
        count_b = count_b + partial_v[e, 1:2]
    count_v[...] = jnp.where(row == 0, count_a, count_b)
    counting = pltpu.make_async_copy(count_v, count_s, sem_local.at[5])
    counting.start()
    counting.wait()

    def gather(s, before, step, primal):
        c, h = s
        for copy in q_copies[s]:
            copy.wait_recv()
        for copy in before:
            copy.wait_send()
        grid = bufs["grid", s]
        for e in (1, 3, 2, 0):
            back = 0 if e == 0 else RING - e
            t = table_of(h, back)

            def one(slot, primal):
                place = table_s[t, 4 + h, slot]
                value = grid[place]
                if e:
                    bufs["back", s][e - 1, slot] = value
                else:
                    bufs["own", s][slot] = value
                if step:
                    sent = bufs["got", s][back - 1, slot] if e else bufs["send", s][c1[h], slot]
                    if step == 1:
                        bufs["held", s][e, slot] = sent - value
                    else:
                        alive = jnp.where(place < n_pos, 1.0, 0.0).astype(jnp.float32)
                        gap = sent - bufs["held", s][e, slot] - value
                        primal = primal + alive * (gap * gap)
                return primal

            primal = lax.fori_loop(0, nb, one, primal, unroll=4)
        return primal

    def back_send(s):
        c, h = s
        copies = []
        for e in (1, 3, 2):
            copy = remote(
                bufs["back", s].at[e - 1], bufs["fetched", s].at[e - 1], sem_w, (c, h, e - 1), first(h, e)
            )
            copy.start()
            copies.append(copy)
        return copies

    def update(c, step):
        cols = pl.ds(c * LANES, LANES)

        def one(slot, total):
            alive = live(slot)
            for h in range(2):
                s = (c, h)
                for e in range(RING):
                    p = lax.rem(c1[h] - e + RING, RING)
                    value = bufs["own", s][slot] if e == 0 else bufs["fetched", s][e - 1, slot]
                    in_block = pl.ds(pl.multiple_of(h * RING * ROWS + p * ROWS, ROWS), ROWS)
                    old = dual[slot, in_block, cols]
                    at = pl.ds(pl.multiple_of(slot * BLOCK + h * RING * ROWS + p * ROWS, ROWS), ROWS)
                    if step > 0:
                        gap = state[at, cols] - value
                        if step < ITERS:
                            total = total + alive * (gap * gap)
                        old = old + alive * gap
                        dual[slot, in_block, cols] = old
                    if step < ITERS:
                        drive[at, cols] = (penalty * alive * (value - old)).astype(jnp.bfloat16)
            return total

        return lax.fori_loop(0, nb, one, jnp.zeros((ROWS, LANES), jnp.float32))

    slots_at_once = 4
    chunk = slots_at_once * BLOCK

    def couple_send(c, step):
        cols = pl.ds(c * LANES, LANES)
        for h in range(2):
            for copy in v_copies.get((c, h), ()):
                copy.wait_send()

        def one(i, _):
            at = pl.ds(pl.multiple_of(i * chunk, chunk), chunk)
            rows = base[at, cols] + jnp.dot(
                kkt[at, 0:bound], drive[:, cols], preferred_element_type=jnp.float32
            )
            state[at, cols] = rows
            for j in range(slots_at_once):
                slot = i * slots_at_once + j
                v = rows[j * BLOCK : (j + 1) * BLOCK] + dual[slot, :, cols]
                for h in range(2):
                    for p in range(RING):
                        lo = h * RING * ROWS + p * ROWS
                        bufs["send", (c, h)][p, slot] = v[lo : lo + ROWS]
            return 0

        lax.fori_loop(0, nb // slots_at_once, one, 0)
        for h in range(2):
            s = (c, h)
            copies = []
            for e in (1, 3, 2):
                p = ring_add(c1[h], e)
                copy = remote(
                    bufs["send", s].at[p, pl.ds(0, nb)], bufs["got", s].at[e - 1, pl.ds(0, nb)],
                    sem_v, (c, h, e - 1), first(h, e),
                )
                copy.start()
                copies.append(copy)
            v_copies[s] = copies

    def reduce_send(s):
        c, h = s
        for copy in v_copies[s]:
            copy.wait_recv()
        for copy in p_copies.get(s, ()):
            copy.wait_send()
        mine_at = c1[h]

        def one(pos, _):
            t = table_of(h, 0)
            value = bufs["send", s][mine_at, table_s[t, 2 * h, pos]] + bufs["send", s][mine_at, table_s[t, 2 * h + 1, pos]]
            for e in range(1, RING):
                t = table_of(h, e)
                value = value + bufs["got", s][e - 1, table_s[t, 2 * h, pos]]
                value = value + bufs["got", s][e - 1, table_s[t, 2 * h + 1, pos]]
            bufs["psum", s][pos] = value
            return 0

        lax.fori_loop(0, n_pos, one, 0, unroll=4)
        copies = []
        for e in (1, 3, 2):
            p = ring_add(c2[h], e)
            copy = remote(
                bufs["psum", s].at[pl.ds(pl.multiple_of(p * mine, mine), mine)], bufs["got2", s].at[e - 1],
                sem_p, (c, h, e - 1), second(h, e),
            )
            copy.start()
            copies.append(copy)
        p_copies[s] = copies

    def renew_send(s, moved):
        c, h = s
        for copy in p_copies[s]:
            copy.wait_recv()
        for copy in q_copies[s]:
            copy.wait_send()
        for k in range(mine):
            at = c2[h] * mine + k
            total = bufs["psum", s][at]
            for e in range(1, RING):
                total = total + bufs["got2", s][e - 1, k]
            count = count_s[h, at]
            new = total / jnp.maximum(count, 1.0)
            change = new - bufs["grid", s][at]
            moved = moved + count * (change * change)
            bufs["grid", s][at] = new
        q_copies[s] = send_grid(s)
        return moved

    for s in streams:
        gather(s, (), 0, zero)
        w_copies[s] = back_send(s)
    primal = [zero] * ITERS
    moved = [zero] * ITERS
    owner_copies = []
    for step in range(ITERS):
        last = step == ITERS - 1
        for c in range(2):
            for h in range(2):
                for copy in w_copies[c, h]:
                    copy.wait_recv()
            got = update(c, step)
            if step > 0:
                primal[step - 1] = primal[step - 1] + got
            couple_send(c, step)
        if last:
            tail = pl.ds(bound, kkt.shape[0] - bound)
            state[tail] = base[tail] + jnp.dot(
                kkt[tail, 0:bound], drive[...], preferred_element_type=jnp.float32
            )
        for s in streams:
            reduce_send(s)
        for s in streams:
            moved[step] = renew_send(s, moved[step])
            if last:
                c, h = s
                for e in range(1, RING):
                    p = ring_add(c1[h], e)
                    at = pl.multiple_of(c2[h] * mine + p * owned, owned)
                    rows = pl.ds(pl.multiple_of(h * RING * ROWS + c1[h] * ROWS, ROWS), ROWS)
                    copy = remote(
                        bufs["grid", s].at[pl.ds(at, owned)], cons.at[:, rows, pl.ds(c * LANES, LANES)],
                        sem_o, (c, h, e - 1), first(h, e),
                    )
                    copy.start()
                    owner_copies.append(copy)
                rows = pl.ds(pl.multiple_of(h * RING * ROWS + c1[h] * ROWS, ROWS), ROWS)
                for o in range(owned):
                    cons[o, rows, c * LANES : (c + 1) * LANES] = bufs["grid", s][c2[h] * mine + c1[h] * owned + o]
        for c in range(2):
            for h in range(2):
                s = (c, h)
                primal[step] = gather(s, w_copies[s], step + 1, primal[step])
                if not (last and c == 1):
                    w_copies[s] = back_send(s)

    tile = jnp.zeros((8, LANES), jnp.float32)
    for step in range(ITERS):
        tile = jnp.where(row == 2 * step, jnp.sum(primal[step], axis=0, keepdims=True), tile)
        change = (penalty * penalty) * jnp.sum(moved[step], axis=0, keepdims=True)
        tile = jnp.where(row == 2 * step + 1, change, tile)
    totals_a[pl.ds(r, 1)] = tile[None]
    norm_copies = []
    for e in range(1, n_region):
        copy = remote(totals_a.at[r], totals_a.at[r], sem_n, (e - 1,), lax.rem(r + e, n_region))
        copy.start()
        norm_copies.append(copy)
    for h in range(2):
        w_copies[1, h] = back_send((1, h))
    for copy in norm_copies:
        copy.wait()
    totals_b[pl.ds(sub, 1)] = jnp.sum(totals_a[...], axis=0, keepdims=True)
    norm_copies = []
    for e in range(1, n_sub):
        copy = pltpu.make_async_remote_copy(
            src_ref=totals_b.at[sub], dst_ref=totals_b.at[sub],
            send_sem=sem_n.at[0, n_region - 2 + e], recv_sem=sem_n.at[1, n_region - 2 + e],
            device_id={"sub": lax.rem(sub + e, n_sub)}, device_id_type=MESH,
        )
        copy.start()
        norm_copies.append(copy)

    for copy in owner_copies:
        copy.wait()
    consensus[...] = cons[...]
    for c in range(2):
        for h in range(2):
            for copy in w_copies[c, h]:
                copy.wait_recv()
        update(c, ITERS)
    for copy in norm_copies:
        copy.wait()
    table = jnp.sum(jnp.sum(totals_b[...], axis=0), axis=1, keepdims=True)
    scale = 1.0 / (n_region * n_sub * 2 * LANES * BLOCK)
    table = jnp.sqrt(table * scale)
    small = (ITERS, 2)
    which = lax.broadcasted_iota(jnp.int32, small, 0) * 2 + lax.broadcasted_iota(jnp.int32, small, 1)
    norms = jnp.zeros(small, jnp.float32)
    for q in range(2 * ITERS):
        norms = jnp.where(which == q, jnp.broadcast_to(table[q : q + 1], small), norms)
    norms_ref[...] = norms

    for s in streams:
        for copy in v_copies[s] + p_copies[s] + q_copies[s] + w_copies[s]:
            copy.wait_send()


def put_out(*refs):
    *arrays, sems = refs
    count = len(arrays) // 2
    copies = [pltpu.make_async_copy(arrays[i], arrays[count + i], sems.at[i]) for i in range(count)]
    for copy in copies:
        copy.start()
    for copy in copies:
        copy.wait()


def shards(kkt_inverse, cost_terms, dual_start, consensus_start, block_target):
    order, scen = cost_terms.shape
    nb = block_target.shape[1]
    owned = consensus_start.shape[0] // BLOCK
    n_region = RING * RING
    n_sub = lax.axis_size("sub")
    n_pos = n_region * owned
    mine = RING * owned
    f32 = jnp.float32
    dma = pltpu.SemaphoreType.DMA
    per_stream = [
        pltpu.VMEM((RING, nb + 1, ROWS, LANES), f32),
        pltpu.VMEM((RING - 1, nb + 1, ROWS, LANES), f32),
        pltpu.VMEM((n_pos, ROWS, LANES), f32),
        pltpu.VMEM((RING - 1, mine, ROWS, LANES), f32),
        pltpu.VMEM((n_pos + 1, ROWS, LANES), f32),
        pltpu.VMEM((RING - 1, nb, ROWS, LANES), f32),
        pltpu.VMEM((RING - 1, nb, ROWS, LANES), f32),
        pltpu.VMEM((nb, ROWS, LANES), f32),
        pltpu.VMEM((RING, nb, ROWS, LANES), f32),
    ]
    state, duals, consensus, norms = pl.pallas_call(
        kernel,
        out_shape=(
            pltpu.VMEM((order, scen), f32),
            pltpu.VMEM((nb, BLOCK, scen), f32),
            pltpu.VMEM((owned, BLOCK, scen), f32),
            pltpu.VMEM((ITERS, 2), f32),
        ),
        in_specs=[pl.BlockSpec(memory_space=pltpu.HBM)] * 4 + [pl.BlockSpec(memory_space=pltpu.SMEM)],
        out_specs=(pl.BlockSpec(memory_space=pltpu.VMEM),) * 4,
        scratch_shapes=[
            pltpu.VMEM((order, order), jnp.bfloat16),
            pltpu.VMEM((order, scen), jnp.bfloat16),
            pltpu.VMEM((order, scen), f32),
            pltpu.VMEM((owned, BLOCK, scen), f32),
            pltpu.VMEM((nb * BLOCK, scen), jnp.bfloat16),
            pltpu.VMEM((2 * RING - 1, 8, LANES), jnp.int32),
            pltpu.SMEM((2 * RING - 1, 8, LANES), jnp.int32),
            pltpu.VMEM((2 * RING - 1, 8, LANES), f32),
            pltpu.VMEM((8, LANES), f32),
            pltpu.SMEM((8, LANES), f32),
            pltpu.VMEM((n_region, 8, LANES), f32),
            pltpu.VMEM((n_sub, 8, LANES), f32),
        ]
        + per_stream * 4
        + [
            dma((6,)),
            dma((2, 2 * RING - 1)),
            dma((2, 2 * RING - 1)),
            dma((2, 2, 2, RING - 1)),
            dma((2, 2, 2, RING - 1)),
            dma((2, 2, 2, RING - 1)),
            dma((2, 2, 2, RING - 1)),
            dma((2, 2, 2, RING - 1)),
            dma((2, 2, 2, RING - 1)),
            dma((2, n_region - 1 + n_sub - 1)),
        ],
        compiler_params=pltpu.CompilerParams(
            collective_id=0, has_side_effects=True, vmem_limit_bytes=40 * 2**20
        ),
        name="admm",
    )(
        *(
            pltpu.with_memory_space_constraint(a, pltpu.HBM)
            for a in (
                kkt_inverse,
                cost_terms,
                dual_start.reshape(nb, BLOCK, scen),
                consensus_start.reshape(owned, BLOCK, scen),
                block_target,
            )
        )
    )
    results = (
        state,
        duals.reshape(nb * BLOCK, scen),
        consensus.reshape(owned * BLOCK, scen),
        norms,
    )
    return pl.pallas_call(
        put_out,
        out_shape=tuple(jax.ShapeDtypeStruct(a.shape, a.dtype) for a in results),
        in_specs=[pl.BlockSpec(memory_space=pltpu.VMEM)] * len(results),
        out_specs=(pl.BlockSpec(memory_space=pl.ANY),) * len(results),
        scratch_shapes=[dma((len(results),))],
        name="put_out",
        compiler_params=pltpu.CompilerParams(vmem_limit_bytes=8 * 2**20),
    )(*(pltpu.with_memory_space_constraint(a, pltpu.VMEM) for a in results))


def solution(mesh):
    both = P(("region", "sub"), None)
    return jax.shard_map(
        shards, mesh=mesh, in_specs=(both,) * 5, out_specs=(both, both, both, P()), check_vma=False
    )
```

```python
import functools

import jax
import jax.numpy as jnp
from jax import lax
from jax.experimental import pallas as pl
from jax.experimental.pallas import tpu as pltpu
from jax.sharding import PartitionSpec as P

MESH = pl.DeviceIdType.MESH
BLOCK = 128
ITERS = 2
RING = 4
QUARTERS = 4
ROWS = 8
LANES = 128
penalty = 1.5


def ring_add(a, e):
    return lax.rem(a + e, RING)


def kernel(
    kkt_ref, cost_ref, dual_ref, cons_ref, target_hbm,
    state, dual, consensus, norms_ref,
    target_ref, kkt, cost, base, cons, drive, tables, table_s, partial_v, count_v, count_s, totals_a, totals_b,
    *rest,
):
    nb = target_hbm.shape[1]
    owned = cons_ref.shape[0]
    n_region = RING * RING
    n_sub = lax.axis_size("sub")
    n_pos = n_region * owned
    mine = RING * owned
    bound = nb * BLOCK
    streams = [(c, q) for c in range(2) for q in range(QUARTERS)]
    bufs = {}
    names = ("send", "got", "psum", "got2", "grid", "back", "fetched", "held")
    rest = list(rest)
    for s in streams:
        for name in names:
            bufs[name, s] = rest.pop(0)
    sem_local, sem_table, sem_count, sem_init, sem_v, sem_p, sem_q, sem_w, sem_o, sem_n = rest

    r = lax.axis_index("region")
    sub = lax.axis_index("sub")
    x = r // RING
    z = lax.rem(r, RING)

    def first(h, e):
        return ring_add(x, e) * RING + z if h == 0 else x * RING + ring_add(z, e)

    def second(h, e):
        return first(1 - h, e)

    c1 = (x, z)
    c2 = (z, x)

    def remote(src, dst, sems, index, region):
        return pltpu.make_async_remote_copy(
            src_ref=src, dst_ref=dst, send_sem=sems.at[(0, *index)], recv_sem=sems.at[(1, *index)],
            device_id={"region": region}, device_id_type=MESH,
        )

    local = [
        pltpu.make_async_copy(target_hbm, target_ref, sem_local.at[6]),
        pltpu.make_async_copy(cons_ref, cons, sem_local.at[0]),
        pltpu.make_async_copy(cost_ref, cost, sem_local.at[1]),
        pltpu.make_async_copy(dual_ref, dual, sem_local.at[2]),
        pltpu.make_async_copy(kkt_ref, kkt, sem_local.at[3]),
    ]
    for copy in local[:2]:
        copy.start()

    barrier = pltpu.get_barrier_semaphore()
    near = [(h, e) for h in range(2) for e in range(1, RING)]
    for h, e in near:
        pl.semaphore_signal(barrier, inc=1, device_id={"region": first(h, e)}, device_id_type=MESH)
    for e in range(1, n_sub):
        pl.semaphore_signal(barrier, inc=1, device_id={"sub": lax.rem(sub + e, n_sub)}, device_id_type=MESH)

    local[0].wait()
    lane = lax.broadcasted_iota(jnp.int32, (8, LANES), 1)
    row = lax.broadcasted_iota(jnp.int32, (8, LANES), 0)
    none = jnp.full((8, LANES), nb, jnp.int32)
    one_a, one_b, two_a, two_b = none, none, none, none
    places = jnp.full((8, LANES), n_pos, jnp.int32)
    for s in range(nb):
        t = target_ref[0, s]
        pos_b = t
        pos_a = lax.rem(t // owned, RING) * mine + (t // (owned * RING)) * owned + lax.rem(t, owned)
        pos_a = jnp.where(t >= 0, pos_a, -1)
        hit_a = lane == pos_a
        hit_b = lane == pos_b
        two_a = jnp.where(hit_a & (one_a < nb), s, two_a)
        one_a = jnp.where(hit_a & (one_a == nb), s, one_a)
        two_b = jnp.where(hit_b & (one_b < nb), s, two_b)
        one_b = jnp.where(hit_b & (one_b == nb), s, one_b)
        here = jnp.where(row == 4, pos_a, pos_b)
        places = jnp.where((lane == s) & (t >= 0), here, places)
    tile = jnp.where(row == 0, one_a, places)
    tile = jnp.where(row == 1, two_a, tile)
    tile = jnp.where(row == 2, one_b, tile)
    tile = jnp.where(row == 3, two_b, tile)
    tables[0] = tile

    zero = jnp.zeros((ROWS, LANES), jnp.float32)
    for s in streams:
        for p in range(RING):
            bufs["send", s][p, nb] = zero
        for p in range(RING - 1):
            bufs["got", s][p, nb] = zero
        bufs["grid", s][n_pos] = zero

    local[1].wait()
    pl.semaphore_wait(barrier, len(near) + n_sub - 1)

    def shard_rows(q, p):
        return pl.ds(pl.multiple_of((q * RING + p) * ROWS, ROWS), ROWS)

    init = {}
    for s in streams:
        c, q = s
        h = q % 2
        for e in range(1, RING):
            p = ring_add(c1[h], e)
            at = pl.multiple_of(c2[h] * mine + c1[h] * owned, owned)
            src = cons.at[:, shard_rows(q, p), pl.ds(c * LANES, LANES)]
            init[s, e] = remote(src, bufs["grid", s].at[pl.ds(at, owned)], sem_init, (c, q, e - 1), first(h, e))
            init[s, e].start()
    table_copies = []
    for h, e in near:
        i = (RING - 1) * h + e
        copy = remote(tables.at[0], tables.at[i], sem_table, (i,), first(h, e))
        copy.start()
        table_copies.append(copy)
    for copy in local[2:]:
        copy.start()
    for s in streams:
        c, q = s
        h = q % 2
        for o in range(owned):
            at = c2[h] * mine + c1[h] * owned + o
            bufs["grid", s][at] = cons[o, shard_rows(q, c1[h]), c * LANES : (c + 1) * LANES]

    def send_grid(s):
        c, q = s
        h = q % 2
        copies = []
        at = pl.ds(pl.multiple_of(c2[h] * mine, mine), mine)
        for e in range(1, RING):
            copy = remote(
                bufs["grid", s].at[at], bufs["grid", s].at[at], sem_q, (c, q, e - 1), second(h, e)
            )
            copy.start()
            copies.append(copy)
        return copies

    q_copies, w_copies, v_copies, p_copies = {}, {}, {}, {}
    for s in streams:
        for e in range(1, RING):
            init[s, e].wait()
        q_copies[s] = send_grid(s)

    for copy in table_copies:
        copy.wait()
    to_scalar = pltpu.make_async_copy(tables, table_s, sem_local.at[4])
    to_scalar.start()

    def uses(i, h):
        hits = (tables[i] < nb).astype(jnp.float32)
        return hits[2 * h : 2 * h + 1] + hits[2 * h + 1 : 2 * h + 2]

    over = []
    for h in range(2):
        total = uses(0, h)
        for e in range(1, RING):
            total = total + uses((RING - 1) * h + e, h)
        over.append(total)
    partial_v[0] = jnp.where(row == 0, over[0], over[1])
    count_copies = []
    for h, e in near:
        i = (RING - 1) * h + e
        copy = remote(partial_v.at[0], partial_v.at[i], sem_count, (i,), first(h, e))
        copy.start()
        count_copies.append(copy)
    to_scalar.wait()

    def table_of(h, e):
        return 0 if e == 0 else (RING - 1) * h + e

    def live(s):
        return jnp.where(target_ref[0, s] >= 0, 1.0, 0.0).astype(jnp.float32)

    def gather(s, before, step, primal):
        c, q = s
        h = q % 2
        for copy in q_copies[s]:
            copy.wait_recv()
        for copy in before:
            copy.wait_send()
        grid = bufs["grid", s]
        for e in (1, 3, 2, 0):
            back = 0 if e == 0 else RING - e
            t = table_of(h, back)

            def one(slot, primal):
                place = table_s[t, 4 + h, slot]
                value = grid[place]
                if e:
                    bufs["back", s][e - 1, slot] = value
                else:
                    bufs["fetched", s][0, slot] = value
                if step:
                    sent = bufs["got", s][back - 1, slot] if e else bufs["send", s][c1[h], slot]
                    if step == 1:
                        bufs["held", s][e, slot] = sent - value
                    else:
                        alive = jnp.where(place < n_pos, 1.0, 0.0).astype(jnp.float32)
                        gap = sent - bufs["held", s][e, slot] - value
                        primal = primal + alive * (gap * gap)
                return primal

            primal = lax.fori_loop(0, nb, one, primal, unroll=4)
        return primal

    def back_send(s):
        c, q = s
        h = q % 2
        copies = []
        for e in (1, 3, 2):
            copy = remote(
                bufs["back", s].at[e - 1], bufs["fetched", s].at[e], sem_w, (c, q, e - 1), first(h, e)
            )
            copy.start()
            copies.append(copy)
        return copies

    def update(c, step):
        cols = pl.ds(c * LANES, LANES)

        def one(slot, total):
            alive = live(slot)
            for q in range(QUARTERS):
                for p in range(0, RING, 2):
                    value = jnp.concatenate(
                        [bufs["fetched", (c, q)][lax.rem(c1[q % 2] - p - i + RING, RING), slot] for i in range(2)]
                    )
                    lo = (q * RING + p) * ROWS
                    in_block = pl.ds(lo, 2 * ROWS)
                    old = dual[slot, in_block, cols]
                    at = pl.ds(pl.multiple_of(slot * BLOCK + lo, 2 * ROWS), 2 * ROWS)
                    if step > 0:
                        gap = state[at, cols] - value
                        if step < ITERS:
                            total = total + alive * (gap * gap)
                        old = old + alive * gap
                        dual[slot, in_block, cols] = old
                    if step < ITERS:
                        drive[at, cols] = (penalty * alive * (value - old)).astype(jnp.bfloat16)
            return total

        total = lax.fori_loop(0, nb, one, jnp.zeros((2 * ROWS, LANES), jnp.float32))
        return total[:ROWS] + total[ROWS:]

    slots_at_once = 4
    chunk = slots_at_once * BLOCK

    def sent(s, e, slots):
        c, q = s
        h = q % 2
        return remote(
            bufs["send", s].at[ring_add(c1[h], e), slots], bufs["got", s].at[e - 1, slots],
            sem_v, (c, q, e - 1), first(h, e),
        )

    def couple_send(c, step):
        cols = pl.ds(c * LANES, LANES)
        for q in range(QUARTERS):
            for copy in v_copies.get((c, q), ()):
                copy.wait_send()

        def one(i, _):
            at = pl.ds(pl.multiple_of(i * chunk, chunk), chunk)
            rows = base[at, cols] + jnp.dot(
                kkt[at, 0:bound], drive[:, cols], preferred_element_type=jnp.float32
            )
            state[at, cols] = rows
            for j in range(slots_at_once):
                slot = i * slots_at_once + j
                v = rows[j * BLOCK : (j + 1) * BLOCK] + dual[slot, :, cols]
                for q in range(QUARTERS):
                    for p in range(RING):
                        lo = (q * RING + p) * ROWS
                        bufs["send", (c, q)][p, slot] = v[lo : lo + ROWS]
            for q in range(QUARTERS):
                for e in (1, 3, 2):
                    sent((c, q), e, pl.ds(i * slots_at_once, slots_at_once)).start()
            return 0

        lax.fori_loop(0, nb // slots_at_once, one, 0)
        for q in range(QUARTERS):
            v_copies[c, q] = [sent((c, q), e, pl.ds(0, nb)) for e in (1, 3, 2)]

    def reduce_send(s):
        c, q = s
        h = q % 2
        for copy in v_copies[s]:
            copy.wait_recv()
        for copy in p_copies.get(s, ()):
            copy.wait_send()
        mine_at = c1[h]

        def one(pos, _):
            t = table_of(h, 0)
            value = bufs["send", s][mine_at, table_s[t, 2 * h, pos]] + bufs["send", s][mine_at, table_s[t, 2 * h + 1, pos]]
            for e in range(1, RING):
                t = table_of(h, e)
                value = value + bufs["got", s][e - 1, table_s[t, 2 * h, pos]]
                value = value + bufs["got", s][e - 1, table_s[t, 2 * h + 1, pos]]
            bufs["psum", s][pos] = value
            return 0

        lax.fori_loop(0, n_pos, one, 0, unroll=8)
        copies = []
        for e in (1, 3, 2):
            p = ring_add(c2[h], e)
            copy = remote(
                bufs["psum", s].at[pl.ds(pl.multiple_of(p * mine, mine), mine)], bufs["got2", s].at[e - 1],
                sem_p, (c, q, e - 1), second(h, e),
            )
            copy.start()
            copies.append(copy)
        p_copies[s] = copies

    def renew_send(s, moved):
        c, q = s
        h = q % 2
        for copy in p_copies[s]:
            copy.wait_recv()
        for copy in q_copies[s]:
            copy.wait_send()
        for k in range(mine):
            at = c2[h] * mine + k
            total = bufs["psum", s][at]
            for e in range(1, RING):
                total = total + bufs["got2", s][e - 1, k]
            count = count_s[h, at]
            new = total / jnp.maximum(count, 1.0)
            change = new - bufs["grid", s][at]
            moved = moved + count * (change * change)
            bufs["grid", s][at] = new
        q_copies[s] = send_grid(s)
        return moved

    for s in streams:
        gather(s, (), 0, zero)
        w_copies[s] = back_send(s)
    local[2].wait()
    local[4].wait()

    half = 256

    def base_rows(i, _):
        at = pl.ds(pl.multiple_of(i * half, half), half)
        base[at] = jnp.dot(kkt[at], cost[...], preferred_element_type=jnp.float32)
        return 0

    lax.fori_loop(0, kkt.shape[0] // half, base_rows, 0)
    local[3].wait()

    for copy in count_copies:
        copy.wait()
    count_a = partial_v[0, 0:1] + partial_v[RING, 0:1]
    count_b = partial_v[0, 1:2] + partial_v[1, 1:2]
    for e in range(2, RING):
        count_a = count_a + partial_v[RING - 1 + e, 0:1]
        count_b = count_b + partial_v[e, 1:2]
    count_v[...] = jnp.where(row == 0, count_a, count_b)
    counting = pltpu.make_async_copy(count_v, count_s, sem_local.at[5])
    counting.start()
    counting.wait()

    primal = [zero] * ITERS
    moved = [zero] * ITERS
    owner_copies = []
    for step in range(ITERS):
        last = step == ITERS - 1
        for c in range(2):
            for q in range(QUARTERS):
                for copy in w_copies[c, q]:
                    copy.wait_recv()
            got = update(c, step)
            if step > 0:
                primal[step - 1] = primal[step - 1] + got
            couple_send(c, step)
        if last:
            tail = pl.ds(bound, kkt.shape[0] - bound)
            state[tail] = base[tail] + jnp.dot(
                kkt[tail, 0:bound], drive[...], preferred_element_type=jnp.float32
            )
        for s in streams:
            reduce_send(s)
        for s in streams:
            moved[step] = renew_send(s, moved[step])
            if last:
                c, q = s
                h = q % 2
                for e in range(1, RING):
                    p = ring_add(c1[h], e)
                    at = pl.multiple_of(c2[h] * mine + p * owned, owned)
                    copy = remote(
                        bufs["grid", s].at[pl.ds(at, owned)],
                        cons.at[:, shard_rows(q, c1[h]), pl.ds(c * LANES, LANES)],
                        sem_o, (c, q, e - 1), first(h, e),
                    )
                    copy.start()
                    owner_copies.append(copy)
                for o in range(owned):
                    at = c2[h] * mine + c1[h] * owned + o
                    cons[o, shard_rows(q, c1[h]), c * LANES : (c + 1) * LANES] = bufs["grid", s][at]
        for c in range(2):
            for q in range(QUARTERS):
                s = (c, q)
                primal[step] = gather(s, w_copies[s], step + 1, primal[step])
                if not (last and c == 1):
                    w_copies[s] = back_send(s)

    tile = jnp.zeros((8, LANES), jnp.float32)
    for step in range(ITERS):
        tile = jnp.where(row == 2 * step, jnp.sum(primal[step], axis=0, keepdims=True), tile)
        change = (penalty * penalty) * jnp.sum(moved[step], axis=0, keepdims=True)
        tile = jnp.where(row == 2 * step + 1, change, tile)
    totals_a[pl.ds(r, 1)] = tile[None]
    norm_copies = []
    for e in range(1, n_region):
        copy = remote(totals_a.at[r], totals_a.at[r], sem_n, (e - 1,), lax.rem(r + e, n_region))
        copy.start()
        norm_copies.append(copy)
    for q in range(QUARTERS):
        w_copies[1, q] = back_send((1, q))
    for copy in norm_copies:
        copy.wait()
    totals_b[pl.ds(sub, 1)] = jnp.sum(totals_a[...], axis=0, keepdims=True)
    norm_copies = []
    for e in range(1, n_sub):
        copy = pltpu.make_async_remote_copy(
            src_ref=totals_b.at[sub], dst_ref=totals_b.at[sub],
            send_sem=sem_n.at[0, n_region - 2 + e], recv_sem=sem_n.at[1, n_region - 2 + e],
            device_id={"sub": lax.rem(sub + e, n_sub)}, device_id_type=MESH,
        )
        copy.start()
        norm_copies.append(copy)

    for copy in owner_copies:
        copy.wait()
    consensus[...] = cons[...]
    for c in range(2):
        for q in range(QUARTERS):
            for copy in w_copies[c, q]:
                copy.wait_recv()
        update(c, ITERS)
    for copy in norm_copies:
        copy.wait()
    table = jnp.sum(jnp.sum(totals_b[...], axis=0), axis=1, keepdims=True)
    scale = 1.0 / (n_region * n_sub * 2 * LANES * BLOCK)
    table = jnp.sqrt(table * scale)
    small = (ITERS, 2)
    which = lax.broadcasted_iota(jnp.int32, small, 0) * 2 + lax.broadcasted_iota(jnp.int32, small, 1)
    norms = jnp.zeros(small, jnp.float32)
    for q in range(2 * ITERS):
        norms = jnp.where(which == q, jnp.broadcast_to(table[q : q + 1], small), norms)
    norms_ref[...] = norms

    for s in streams:
        for copy in v_copies[s] + p_copies[s] + q_copies[s] + w_copies[s]:
            copy.wait_send()


def put_out(*refs):
    *arrays, sems = refs
    count = len(arrays) // 2
    copies = [pltpu.make_async_copy(arrays[i], arrays[count + i], sems.at[i]) for i in range(count)]
    for copy in copies:
        copy.start()
    for copy in copies:
        copy.wait()


def shards(kkt_inverse, cost_terms, dual_start, consensus_start, block_target):
    order, scen = cost_terms.shape
    nb = block_target.shape[1]
    owned = consensus_start.shape[0] // BLOCK
    n_region = RING * RING
    n_sub = lax.axis_size("sub")
    n_pos = n_region * owned
    mine = RING * owned
    f32 = jnp.float32
    dma = pltpu.SemaphoreType.DMA
    per_stream = [
        pltpu.VMEM((RING, nb + 1, ROWS, LANES), f32),
        pltpu.VMEM((RING - 1, nb + 1, ROWS, LANES), f32),
        pltpu.VMEM((n_pos, ROWS, LANES), f32),
        pltpu.VMEM((RING - 1, mine, ROWS, LANES), f32),
        pltpu.VMEM((n_pos + 1, ROWS, LANES), f32),
        pltpu.VMEM((RING - 1, nb, ROWS, LANES), f32),
        pltpu.VMEM((RING, nb, ROWS, LANES), f32),
        pltpu.VMEM((RING, nb, ROWS, LANES), f32),
    ]
    state, duals, consensus, norms = pl.pallas_call(
        kernel,
        out_shape=(
            pltpu.VMEM((order, scen), f32),
            pltpu.VMEM((nb, BLOCK, scen), f32),
            pltpu.VMEM((owned, BLOCK, scen), f32),
            pltpu.VMEM((ITERS, 2), f32),
        ),
        in_specs=[pl.BlockSpec(memory_space=pltpu.HBM)] * 5,
        out_specs=(pl.BlockSpec(memory_space=pltpu.VMEM),) * 4,
        scratch_shapes=[
            pltpu.SMEM((1, nb), jnp.int32),
            pltpu.VMEM((order, order), jnp.bfloat16),
            pltpu.VMEM((order, scen), jnp.bfloat16),
            pltpu.VMEM((order, scen), f32),
            pltpu.VMEM((owned, BLOCK, scen), f32),
            pltpu.VMEM((nb * BLOCK, scen), jnp.bfloat16),
            pltpu.VMEM((2 * RING - 1, 8, LANES), jnp.int32),
            pltpu.SMEM((2 * RING - 1, 8, LANES), jnp.int32),
            pltpu.VMEM((2 * RING - 1, 8, LANES), f32),
            pltpu.VMEM((8, LANES), f32),
            pltpu.SMEM((8, LANES), f32),
            pltpu.VMEM((n_region, 8, LANES), f32),
            pltpu.VMEM((n_sub, 8, LANES), f32),
        ]
        + per_stream * (2 * QUARTERS)
        + [
            dma((7,)),
            dma((2, 2 * RING - 1)),
            dma((2, 2 * RING - 1)),
            dma((2, 2, QUARTERS, RING - 1)),
            dma((2, 2, QUARTERS, RING - 1)),
            dma((2, 2, QUARTERS, RING - 1)),
            dma((2, 2, QUARTERS, RING - 1)),
            dma((2, 2, QUARTERS, RING - 1)),
            dma((2, 2, QUARTERS, RING - 1)),
            dma((2, n_region - 1 + n_sub - 1)),
        ],
        compiler_params=pltpu.CompilerParams(
            collective_id=0, has_side_effects=True, vmem_limit_bytes=40 * 2**20
        ),
        name="admm",
    )(
        *(
            pltpu.with_memory_space_constraint(a, pltpu.HBM)
            for a in (
                kkt_inverse,
                cost_terms,
                dual_start.reshape(nb, BLOCK, scen),
                consensus_start.reshape(owned, BLOCK, scen),
                block_target,
            )
        )
    )
    results = (
        state,
        duals.reshape(nb * BLOCK, scen),
        consensus.reshape(owned * BLOCK, scen),
        norms,
    )
    return pl.pallas_call(
        put_out,
        out_shape=tuple(jax.ShapeDtypeStruct(a.shape, a.dtype) for a in results),
        in_specs=[pl.BlockSpec(memory_space=pltpu.VMEM)] * len(results),
        out_specs=(pl.BlockSpec(memory_space=pl.ANY),) * len(results),
        scratch_shapes=[dma((len(results),))],
        name="put_out",
        compiler_params=pltpu.CompilerParams(vmem_limit_bytes=8 * 2**20),
    )(*(pltpu.with_memory_space_constraint(a, pltpu.VMEM) for a in results))


def solution(mesh):
    both = P(("region", "sub"), None)
    return jax.shard_map(
        shards, mesh=mesh, in_specs=(both,) * 5, out_specs=(both, both, both, P()), check_vma=False
    )
```

```python
import functools

import jax
import jax.numpy as jnp
from jax import lax
from jax.experimental import pallas as pl
from jax.experimental.pallas import tpu as pltpu
from jax.sharding import PartitionSpec as P

MESH = pl.DeviceIdType.MESH
BLOCK = 128
ITERS = 2
RING = 4
QUARTERS = 4
ROWS = 8
LANES = 128
penalty = 1.5


def ring_add(a, e):
    return lax.rem(a + e, RING)


def kernel(
    kkt_ref, cost_ref, dual_ref, cons_ref, target_hbm,
    state, dual, consensus, norms_ref,
    target_ref, kkt, cost, base, cons, drive, tables, table_s, partial_v, count_v, count_s, totals_a, totals_b,
    *rest,
):
    nb = target_hbm.shape[1]
    owned = cons_ref.shape[0]
    n_region = RING * RING
    n_sub = lax.axis_size("sub")
    n_pos = n_region * owned
    mine = RING * owned
    bound = nb * BLOCK
    streams = [(c, q) for c in range(2) for q in range(QUARTERS)]
    bufs = {}
    names = ("send", "got", "psum", "got2", "grid", "back", "fetched", "held")
    rest = list(rest)
    for s in streams:
        for name in names:
            bufs[name, s] = rest.pop(0)
    sem_local, sem_table, sem_count, sem_init, sem_v, sem_p, sem_q, sem_w, sem_o, sem_n = rest

    r = lax.axis_index("region")
    sub = lax.axis_index("sub")
    x = r // RING
    z = lax.rem(r, RING)

    def first(h, e):
        return ring_add(x, e) * RING + z if h == 0 else x * RING + ring_add(z, e)

    def second(h, e):
        return first(1 - h, e)

    c1 = (x, z)
    c2 = (z, x)

    def remote(src, dst, sems, index, region):
        return pltpu.make_async_remote_copy(
            src_ref=src, dst_ref=dst, send_sem=sems.at[(0, *index)], recv_sem=sems.at[(1, *index)],
            device_id={"region": region}, device_id_type=MESH,
        )

    def group(ref, sems, index):
        return remote(ref, ref, sems, index, r)

    local = [
        pltpu.make_async_copy(target_hbm, target_ref, sem_local.at[6]),
        pltpu.make_async_copy(cons_ref, cons, sem_local.at[0]),
        pltpu.make_async_copy(cost_ref, cost, sem_local.at[1]),
        pltpu.make_async_copy(dual_ref, dual, sem_local.at[2]),
        pltpu.make_async_copy(kkt_ref, kkt, sem_local.at[3]),
    ]
    for copy in local[:2]:
        copy.start()

    barrier = pltpu.get_barrier_semaphore()
    near = [(h, e) for h in range(2) for e in range(1, RING)]
    for h, e in near:
        pl.semaphore_signal(barrier, inc=1, device_id={"region": first(h, e)}, device_id_type=MESH)
    for e in range(1, n_sub):
        pl.semaphore_signal(barrier, inc=1, device_id={"sub": lax.rem(sub + e, n_sub)}, device_id_type=MESH)

    local[0].wait()
    lane = lax.broadcasted_iota(jnp.int32, (8, LANES), 1)
    row = lax.broadcasted_iota(jnp.int32, (8, LANES), 0)
    none = jnp.full((8, LANES), nb, jnp.int32)
    one_a, one_b, two_a, two_b = none, none, none, none
    places = jnp.full((8, LANES), n_pos, jnp.int32)
    for s in range(nb):
        t = target_ref[0, s]
        pos_b = t
        pos_a = lax.rem(t // owned, RING) * mine + (t // (owned * RING)) * owned + lax.rem(t, owned)
        pos_a = jnp.where(t >= 0, pos_a, -1)
        hit_a = lane == pos_a
        hit_b = lane == pos_b
        two_a = jnp.where(hit_a & (one_a < nb), s, two_a)
        one_a = jnp.where(hit_a & (one_a == nb), s, one_a)
        two_b = jnp.where(hit_b & (one_b < nb), s, two_b)
        one_b = jnp.where(hit_b & (one_b == nb), s, one_b)
        here = jnp.where(row == 4, pos_a, pos_b)
        places = jnp.where((lane == s) & (t >= 0), here, places)
    tile = jnp.where(row == 0, one_a, places)
    tile = jnp.where(row == 1, two_a, tile)
    tile = jnp.where(row == 2, one_b, tile)
    tile = jnp.where(row == 3, two_b, tile)
    tables[0] = tile

    zero = jnp.zeros((ROWS, LANES), jnp.float32)
    for s in streams:
        for p in range(RING):
            bufs["send", s][p, nb] = zero
        for p in range(RING - 1):
            bufs["got", s][p, nb] = zero
        bufs["grid", s][n_pos] = zero

    local[1].wait()
    pl.semaphore_wait(barrier, len(near) + n_sub - 1)

    def shard_rows(q, p):
        return pl.ds(pl.multiple_of((q * RING + p) * ROWS, ROWS), ROWS)

    for s in streams:
        c, q = s
        h = q % 2
        for e in range(1, RING):
            p = ring_add(c1[h], e)
            at = pl.multiple_of(c2[h] * mine + c1[h] * owned, owned)
            src = cons.at[:, shard_rows(q, p), pl.ds(c * LANES, LANES)]
            remote(src, bufs["grid", s].at[pl.ds(at, owned)], sem_init, (c,), first(h, e)).start()
    table_copies = []
    for h, e in near:
        i = (RING - 1) * h + e
        remote(tables.at[0], tables.at[i], sem_table, (), first(h, e)).start()
    table_copies.append(group(tables.at[pl.ds(1, len(near))], sem_table, ()))
    for copy in local[2:]:
        copy.start()
    for s in streams:
        c, q = s
        h = q % 2
        for o in range(owned):
            at = c2[h] * mine + c1[h] * owned + o
            bufs["grid", s][at] = cons[o, shard_rows(q, c1[h]), c * LANES : (c + 1) * LANES]

    def send_grid(s):
        c, q = s
        h = q % 2
        at = pl.ds(pl.multiple_of(c2[h] * mine, mine), mine)
        for e in range(1, RING):
            copy = remote(
                bufs["grid", s].at[at], bufs["grid", s].at[at], sem_q, (c, q), second(h, e)
            )
            copy.start()
        return [group(bufs["grid", s].at[pl.ds(0, (RING - 1) * mine)], sem_q, (c, q))]

    q_copies, w_copies, v_copies, p_copies = {}, {}, {}, {}
    for s in streams:
        if s[1] == 0:
            group(cons.at[:, pl.ds(0, (RING - 1) * QUARTERS * ROWS // 2)], sem_init, (s[0],)).wait()
        q_copies[s] = send_grid(s)

    for copy in table_copies:
        copy.wait()
    to_scalar = pltpu.make_async_copy(tables, table_s, sem_local.at[4])
    to_scalar.start()

    def uses(i, h):
        hits = (tables[i] < nb).astype(jnp.float32)
        return hits[2 * h : 2 * h + 1] + hits[2 * h + 1 : 2 * h + 2]

    over = []
    for h in range(2):
        total = uses(0, h)
        for e in range(1, RING):
            total = total + uses((RING - 1) * h + e, h)
        over.append(total)
    partial_v[0] = jnp.where(row == 0, over[0], over[1])
    count_copies = []
    for h, e in near:
        i = (RING - 1) * h + e
        remote(partial_v.at[0], partial_v.at[i], sem_count, (), first(h, e)).start()
    count_copies.append(group(partial_v.at[pl.ds(1, len(near))], sem_count, ()))
    to_scalar.wait()

    def table_of(h, e):
        return 0 if e == 0 else (RING - 1) * h + e

    def live(s):
        return jnp.where(target_ref[0, s] >= 0, 1.0, 0.0).astype(jnp.float32)

    def gather(s, before, step, primal):
        c, q = s
        h = q % 2
        for copy in q_copies[s]:
            copy.wait_recv()
        for copy in before:
            copy.wait_send()
        grid = bufs["grid", s]
        for e in (1, 3, 2, 0):
            back = 0 if e == 0 else RING - e
            t = table_of(h, back)

            def one(slot, primal):
                place = table_s[t, 4 + h, slot]
                value = grid[place]
                if e:
                    bufs["back", s][e - 1, slot] = value
                else:
                    bufs["fetched", s][0, slot] = value
                if step:
                    sent = bufs["got", s][back - 1, slot] if e else bufs["send", s][c1[h], slot]
                    if step == 1:
                        bufs["held", s][e, slot] = sent - value
                    else:
                        alive = jnp.where(place < n_pos, 1.0, 0.0).astype(jnp.float32)
                        gap = sent - bufs["held", s][e, slot] - value
                        primal = primal + alive * (gap * gap)
                return primal

            primal = lax.fori_loop(0, nb, one, primal, unroll=4)
        return primal

    def back_send(s):
        c, q = s
        h = q % 2
        for e in (1, 3, 2):
            copy = remote(
                bufs["back", s].at[e - 1], bufs["fetched", s].at[e], sem_w, (c, q), first(h, e)
            )
            copy.start()
        return [group(bufs["back", s], sem_w, (c, q))]

    def update(c, q, step):
        cols = pl.ds(c * LANES, LANES)

        def one(slot, total):
            alive = live(slot)
            for p in range(0, RING, 2):
                value = jnp.concatenate(
                    [bufs["fetched", (c, q)][lax.rem(c1[q % 2] - p - i + RING, RING), slot] for i in range(2)]
                )
                lo = (q * RING + p) * ROWS
                in_block = pl.ds(lo, 2 * ROWS)
                old = dual[slot, in_block, cols]
                at = pl.ds(pl.multiple_of(slot * BLOCK + lo, 2 * ROWS), 2 * ROWS)
                if step > 0:
                    gap = state[at, cols] - value
                    if step < ITERS:
                        total = total + alive * (gap * gap)
                    old = old + alive * gap
                    dual[slot, in_block, cols] = old
                if step < ITERS:
                    drive[at, cols] = (penalty * alive * (value - old)).astype(jnp.bfloat16)
            return total

        total = lax.fori_loop(0, nb, one, jnp.zeros((2 * ROWS, LANES), jnp.float32), unroll=4)
        return total[:ROWS] + total[ROWS:]

    slots_at_once = 4
    chunk = slots_at_once * BLOCK

    def sent(s, e, slots):
        c, q = s
        h = q % 2
        return remote(
            bufs["send", s].at[ring_add(c1[h], e), slots], bufs["got", s].at[e - 1, slots],
            sem_v, (c, q), first(h, e),
        )

    def couple_send(c, step):
        cols = pl.ds(c * LANES, LANES)
        for q in range(QUARTERS):
            for copy in v_copies.get((c, q), ()):
                copy.wait_send()

        def one(i, _):
            at = pl.ds(pl.multiple_of(i * chunk, chunk), chunk)
            rows = base[at, cols] + jnp.dot(
                kkt[at, 0:bound], drive[:, cols], preferred_element_type=jnp.float32
            )
            state[at, cols] = rows
            for j in range(slots_at_once):
                slot = i * slots_at_once + j
                v = rows[j * BLOCK : (j + 1) * BLOCK] + dual[slot, :, cols]
                for q in range(QUARTERS):
                    for p in range(RING):
                        lo = (q * RING + p) * ROWS
                        bufs["send", (c, q)][p, slot] = v[lo : lo + ROWS]
            for q in range(QUARTERS):
                for e in (1, 3, 2):
                    sent((c, q), e, pl.ds(i * slots_at_once, slots_at_once)).start()
            return 0

        lax.fori_loop(0, nb // slots_at_once, one, 0)
        for q in range(QUARTERS):
            v_copies[c, q] = [group(bufs["got", (c, q)].at[:, pl.ds(0, nb)], sem_v, (c, q))]

    def reduce_send(s):
        c, q = s
        h = q % 2
        for copy in v_copies[s]:
            copy.wait_recv()
        for copy in p_copies.get(s, ()):
            copy.wait_send()
        mine_at = c1[h]

        def one(pos, _):
            t = table_of(h, 0)
            value = bufs["send", s][mine_at, table_s[t, 2 * h, pos]] + bufs["send", s][mine_at, table_s[t, 2 * h + 1, pos]]
            for e in range(1, RING):
                t = table_of(h, e)
                value = value + bufs["got", s][e - 1, table_s[t, 2 * h, pos]]
                value = value + bufs["got", s][e - 1, table_s[t, 2 * h + 1, pos]]
            bufs["psum", s][pos] = value
            return 0

        lax.fori_loop(0, n_pos, one, 0, unroll=8)
        for e in (1, 3, 2):
            p = ring_add(c2[h], e)
            copy = remote(
                bufs["psum", s].at[pl.ds(pl.multiple_of(p * mine, mine), mine)], bufs["got2", s].at[e - 1],
                sem_p, (c, q), second(h, e),
            )
            copy.start()
        p_copies[s] = [group(bufs["got2", s], sem_p, (c, q))]

    def renew_send(s, moved):
        c, q = s
        h = q % 2
        for copy in p_copies[s]:
            copy.wait_recv()
        for copy in q_copies[s]:
            copy.wait_send()
        for k in range(mine):
            at = c2[h] * mine + k
            total = bufs["psum", s][at]
            for e in range(1, RING):
                total = total + bufs["got2", s][e - 1, k]
            count = count_s[h, at]
            new = total / jnp.maximum(count, 1.0)
            change = new - bufs["grid", s][at]
            moved = moved + count * (change * change)
            bufs["grid", s][at] = new
        q_copies[s] = send_grid(s)
        return moved

    for s in streams:
        gather(s, (), 0, zero)
        w_copies[s] = back_send(s)
    local[2].wait()
    local[4].wait()

    half = 256

    def base_rows(i, _):
        at = pl.ds(pl.multiple_of(i * half, half), half)
        base[at] = jnp.dot(kkt[at], cost[...], preferred_element_type=jnp.float32)
        return 0

    lax.fori_loop(0, kkt.shape[0] // half, base_rows, 0)
    local[3].wait()

    for copy in count_copies:
        copy.wait()
    count_a = partial_v[0, 0:1] + partial_v[RING, 0:1]
    count_b = partial_v[0, 1:2] + partial_v[1, 1:2]
    for e in range(2, RING):
        count_a = count_a + partial_v[RING - 1 + e, 0:1]
        count_b = count_b + partial_v[e, 1:2]
    count_v[...] = jnp.where(row == 0, count_a, count_b)
    counting = pltpu.make_async_copy(count_v, count_s, sem_local.at[5])
    counting.start()
    counting.wait()

    primal = [zero] * ITERS
    moved = [zero] * ITERS
    for step in range(ITERS):
        last = step == ITERS - 1
        for c in range(2):
            for q in range(QUARTERS):
                for copy in w_copies[c, q]:
                    copy.wait_recv()
                got = update(c, q, step)
                if step > 0:
                    primal[step - 1] = primal[step - 1] + got
            couple_send(c, step)
        if last:
            tail = pl.ds(bound, kkt.shape[0] - bound)
            state[tail] = base[tail] + jnp.dot(
                kkt[tail, 0:bound], drive[...], preferred_element_type=jnp.float32
            )
        for s in streams:
            reduce_send(s)
        for s in streams:
            moved[step] = renew_send(s, moved[step])
            if last:
                c, q = s
                h = q % 2
                for e in range(1, RING):
                    p = ring_add(c1[h], e)
                    at = pl.multiple_of(c2[h] * mine + p * owned, owned)
                    copy = remote(
                        bufs["grid", s].at[pl.ds(at, owned)],
                        cons.at[:, shard_rows(q, c1[h]), pl.ds(c * LANES, LANES)],
                        sem_o, (), first(h, e),
                    )
                    copy.start()
                for o in range(owned):
                    at = c2[h] * mine + c1[h] * owned + o
                    cons[o, shard_rows(q, c1[h]), c * LANES : (c + 1) * LANES] = bufs["grid", s][at]
        for c in range(2):
            for q in range(QUARTERS):
                s = (c, q)
                primal[step] = gather(s, w_copies[s], step + 1, primal[step])
                if not (last and c == 1):
                    w_copies[s] = back_send(s)

    tile = jnp.zeros((8, LANES), jnp.float32)
    for step in range(ITERS):
        tile = jnp.where(row == 2 * step, jnp.sum(primal[step], axis=0, keepdims=True), tile)
        change = (penalty * penalty) * jnp.sum(moved[step], axis=0, keepdims=True)
        tile = jnp.where(row == 2 * step + 1, change, tile)
    totals_b[pl.ds(sub, 1)] = tile[None]
    norm_copies = []
    for e in range(1, n_sub):
        copy = pltpu.make_async_remote_copy(
            src_ref=totals_b.at[sub], dst_ref=totals_b.at[sub],
            send_sem=sem_n.at[0, 1], recv_sem=sem_n.at[1, 1],
            device_id={"sub": lax.rem(sub + e, n_sub)}, device_id_type=MESH,
        )
        copy.start()
    norm_copies.append(group(totals_b.at[pl.ds(0, n_sub - 1)], sem_n, (1,)))
    for q in range(QUARTERS - 1):
        w_copies[1, q] = back_send((1, q))
    for copy in norm_copies:
        copy.wait()
    totals_a[pl.ds(r, 1)] = jnp.sum(totals_b[...], axis=0, keepdims=True)
    norm_copies = []
    for e in range(1, n_region):
        remote(totals_a.at[r], totals_a.at[r], sem_n, (0,), lax.rem(r + e, n_region)).start()
    norm_copies.append(group(totals_a.at[pl.ds(0, n_region - 1)], sem_n, (0,)))
    w_copies[1, QUARTERS - 1] = back_send((1, QUARTERS - 1))

    group(cons.at[:, pl.ds(0, (RING - 1) * QUARTERS * ROWS)], sem_o, ()).wait()
    consensus[...] = cons[...]
    for c in range(2):
        for q in range(QUARTERS):
            for copy in w_copies[c, q]:
                copy.wait_recv()
            update(c, q, ITERS)
    for copy in norm_copies:
        copy.wait()
    table = jnp.sum(jnp.sum(totals_a[...], axis=0), axis=1, keepdims=True)
    scale = 1.0 / (n_region * n_sub * 2 * LANES * BLOCK)
    table = jnp.sqrt(table * scale)
    small = (ITERS, 2)
    which = lax.broadcasted_iota(jnp.int32, small, 0) * 2 + lax.broadcasted_iota(jnp.int32, small, 1)
    norms = jnp.zeros(small, jnp.float32)
    for q in range(2 * ITERS):
        norms = jnp.where(which == q, jnp.broadcast_to(table[q : q + 1], small), norms)
    norms_ref[...] = norms

    for s in streams:
        for copy in v_copies[s] + p_copies[s] + q_copies[s] + w_copies[s]:
            copy.wait_send()


def put_out(*refs):
    *arrays, sems = refs
    count = len(arrays) // 2
    copies = [pltpu.make_async_copy(arrays[i], arrays[count + i], sems.at[i]) for i in range(count)]
    for copy in copies:
        copy.start()
    for copy in copies:
        copy.wait()


def shards(kkt_inverse, cost_terms, dual_start, consensus_start, block_target):
    order, scen = cost_terms.shape
    nb = block_target.shape[1]
    owned = consensus_start.shape[0] // BLOCK
    n_region = RING * RING
    n_sub = lax.axis_size("sub")
    n_pos = n_region * owned
    mine = RING * owned
    f32 = jnp.float32
    dma = pltpu.SemaphoreType.DMA
    per_stream = [
        pltpu.VMEM((RING, nb + 1, ROWS, LANES), f32),
        pltpu.VMEM((RING - 1, nb + 1, ROWS, LANES), f32),
        pltpu.VMEM((n_pos, ROWS, LANES), f32),
        pltpu.VMEM((RING - 1, mine, ROWS, LANES), f32),
        pltpu.VMEM((n_pos + 1, ROWS, LANES), f32),
        pltpu.VMEM((RING - 1, nb, ROWS, LANES), f32),
        pltpu.VMEM((RING, nb, ROWS, LANES), f32),
        pltpu.VMEM((RING, nb, ROWS, LANES), f32),
    ]
    state, duals, consensus, norms = pl.pallas_call(
        kernel,
        out_shape=(
            pltpu.VMEM((order, scen), f32),
            pltpu.VMEM((nb, BLOCK, scen), f32),
            pltpu.VMEM((owned, BLOCK, scen), f32),
            pltpu.VMEM((ITERS, 2), f32),
        ),
        in_specs=[pl.BlockSpec(memory_space=pltpu.HBM)] * 5,
        out_specs=(pl.BlockSpec(memory_space=pltpu.VMEM),) * 4,
        scratch_shapes=[
            pltpu.SMEM((1, nb), jnp.int32),
            pltpu.VMEM((order, order), jnp.bfloat16),
            pltpu.VMEM((order, scen), jnp.bfloat16),
            pltpu.VMEM((order, scen), f32),
            pltpu.VMEM((owned, BLOCK, scen), f32),
            pltpu.VMEM((nb * BLOCK, scen), jnp.bfloat16),
            pltpu.VMEM((2 * RING - 1, 8, LANES), jnp.int32),
            pltpu.SMEM((2 * RING - 1, 8, LANES), jnp.int32),
            pltpu.VMEM((2 * RING - 1, 8, LANES), f32),
            pltpu.VMEM((8, LANES), f32),
            pltpu.SMEM((8, LANES), f32),
            pltpu.VMEM((n_region, 8, LANES), f32),
            pltpu.VMEM((n_sub, 8, LANES), f32),
        ]
        + per_stream * (2 * QUARTERS)
        + [
            dma((7,)),
            dma((2,)),
            dma((2,)),
            dma((2, 2)),
            dma((2, 2, QUARTERS)),
            dma((2, 2, QUARTERS)),
            dma((2, 2, QUARTERS)),
            dma((2, 2, QUARTERS)),
            dma((2,)),
            dma((2, 2)),
        ],
        compiler_params=pltpu.CompilerParams(
            collective_id=0, has_side_effects=True, vmem_limit_bytes=40 * 2**20
        ),
        name="admm",
    )(
        *(
            pltpu.with_memory_space_constraint(a, pltpu.HBM)
            for a in (
                kkt_inverse,
                cost_terms,
                dual_start.reshape(nb, BLOCK, scen),
                consensus_start.reshape(owned, BLOCK, scen),
                block_target,
            )
        )
    )
    results = (
        state,
        duals.reshape(nb * BLOCK, scen),
        consensus.reshape(owned * BLOCK, scen),
        norms,
    )
    return pl.pallas_call(
        put_out,
        out_shape=tuple(jax.ShapeDtypeStruct(a.shape, a.dtype) for a in results),
        in_specs=[pl.BlockSpec(memory_space=pltpu.VMEM)] * len(results),
        out_specs=(pl.BlockSpec(memory_space=pl.ANY),) * len(results),
        scratch_shapes=[dma((len(results),))],
        name="put_out",
        compiler_params=pltpu.CompilerParams(vmem_limit_bytes=8 * 2**20),
    )(*(pltpu.with_memory_space_constraint(a, pltpu.VMEM) for a in results))


def solution(mesh):
    both = P(("region", "sub"), None)
    return jax.shard_map(
        shards, mesh=mesh, in_specs=(both,) * 5, out_specs=(both, both, both, P()), check_vma=False
    )
```

```python
import functools

import jax
import jax.numpy as jnp
from jax import lax
from jax.experimental import pallas as pl
from jax.experimental.pallas import tpu as pltpu
from jax.sharding import PartitionSpec as P

MESH = pl.DeviceIdType.MESH
BLOCK = 128
ITERS = 2
RING = 4
QUARTERS = 4
ROWS = 8
LANES = 128
penalty = 1.5


def ring_add(a, e):
    return lax.rem(a + e, RING)


def kernel(
    kkt_ref, cost_ref, dual_ref, cons_ref, target_hbm,
    state, dual, consensus, norms_ref,
    target_ref, kkt, cost, base, cons, drive, tables, table_s, partial_v, count_v, count_s, totals_a, totals_b,
    *rest,
):
    nb = target_hbm.shape[1]
    owned = cons_ref.shape[0]
    n_region = RING * RING
    n_sub = lax.axis_size("sub")
    n_pos = n_region * owned
    mine = RING * owned
    bound = nb * BLOCK
    streams = [(c, q) for c in range(2) for q in range(QUARTERS)]
    bufs = {}
    names = ("send", "got", "psum", "got2", "grid", "back", "fetched")
    rest = list(rest)
    for s in streams:
        for name in names:
            bufs[name, s] = rest.pop(0)
    sem_local, sem_table, sem_count, sem_init, sem_v, sem_p, sem_q, sem_w, sem_o, sem_n = rest

    r = lax.axis_index("region")
    sub = lax.axis_index("sub")
    x = r // RING
    z = lax.rem(r, RING)

    def first(h, e):
        return ring_add(x, e) * RING + z if h == 0 else x * RING + ring_add(z, e)

    def second(h, e):
        return first(1 - h, e)

    c1 = (x, z)
    c2 = (z, x)

    def remote(src, dst, sems, index, region):
        return pltpu.make_async_remote_copy(
            src_ref=src, dst_ref=dst, send_sem=sems.at[(0, *index)], recv_sem=sems.at[(1, *index)],
            device_id={"region": region}, device_id_type=MESH,
        )

    def group(ref, sems, index):
        return remote(ref, ref, sems, index, r)

    local = [
        pltpu.make_async_copy(target_hbm, target_ref, sem_local.at[6]),
        pltpu.make_async_copy(cons_ref, cons, sem_local.at[0]),
        pltpu.make_async_copy(cost_ref, cost, sem_local.at[1]),
        pltpu.make_async_copy(dual_ref, dual, sem_local.at[2]),
        pltpu.make_async_copy(kkt_ref, kkt, sem_local.at[3]),
    ]
    for copy in local[:2]:
        copy.start()

    barrier = pltpu.get_barrier_semaphore()
    near = [(h, e) for h in range(2) for e in range(1, RING)]
    for h, e in near:
        pl.semaphore_signal(barrier, inc=1, device_id={"region": first(h, e)}, device_id_type=MESH)
    for e in range(1, n_sub):
        pl.semaphore_signal(barrier, inc=1, device_id={"sub": lax.rem(sub + e, n_sub)}, device_id_type=MESH)

    local[0].wait()
    lane = lax.broadcasted_iota(jnp.int32, (8, LANES), 1)
    row = lax.broadcasted_iota(jnp.int32, (8, LANES), 0)
    none = jnp.full((8, LANES), nb, jnp.int32)
    one_a, one_b, two_a, two_b = none, none, none, none
    places = jnp.full((8, LANES), n_pos, jnp.int32)
    for s in range(nb):
        t = target_ref[0, s]
        pos_b = t
        pos_a = lax.rem(t // owned, RING) * mine + (t // (owned * RING)) * owned + lax.rem(t, owned)
        pos_a = jnp.where(t >= 0, pos_a, -1)
        hit_a = lane == pos_a
        hit_b = lane == pos_b
        two_a = jnp.where(hit_a & (one_a < nb), s, two_a)
        one_a = jnp.where(hit_a & (one_a == nb), s, one_a)
        two_b = jnp.where(hit_b & (one_b < nb), s, two_b)
        one_b = jnp.where(hit_b & (one_b == nb), s, one_b)
        here = jnp.where(row == 4, pos_a, pos_b)
        places = jnp.where((lane == s) & (t >= 0), here, places)
    tile = jnp.where(row == 0, one_a, places)
    tile = jnp.where(row == 1, two_a, tile)
    tile = jnp.where(row == 2, one_b, tile)
    tile = jnp.where(row == 3, two_b, tile)
    tables[0] = tile

    zero = jnp.zeros((ROWS, LANES), jnp.float32)
    for s in streams:
        for p in range(RING):
            bufs["send", s][p, nb] = zero
        for p in range(RING - 1):
            bufs["got", s][p, nb] = zero
        bufs["grid", s][n_pos] = zero

    local[1].wait()
    pl.semaphore_wait(barrier, len(near) + n_sub - 1)

    def shard_rows(q, p):
        return pl.ds(pl.multiple_of((q * RING + p) * ROWS, ROWS), ROWS)

    for s in streams:
        c, q = s
        h = q % 2
        for e in range(1, RING):
            p = ring_add(c1[h], e)
            at = pl.multiple_of(c2[h] * mine + c1[h] * owned, owned)
            src = cons.at[:, shard_rows(q, p), pl.ds(c * LANES, LANES)]
            remote(src, bufs["grid", s].at[pl.ds(at, owned)], sem_init, (c,), first(h, e)).start()
    table_copies = []
    for h, e in near:
        i = (RING - 1) * h + e
        remote(tables.at[0], tables.at[i], sem_table, (), first(h, e)).start()
    table_copies.append(group(tables.at[pl.ds(1, len(near))], sem_table, ()))
    for copy in local[2:]:
        copy.start()
    for s in streams:
        c, q = s
        h = q % 2
        for o in range(owned):
            at = c2[h] * mine + c1[h] * owned + o
            bufs["grid", s][at] = cons[o, shard_rows(q, c1[h]), c * LANES : (c + 1) * LANES]

    def send_grid(s):
        c, q = s
        h = q % 2
        at = pl.ds(pl.multiple_of(c2[h] * mine, mine), mine)
        for e in range(1, RING):
            copy = remote(
                bufs["grid", s].at[at], bufs["grid", s].at[at], sem_q, (c, q), second(h, e)
            )
            copy.start()
        return [group(bufs["grid", s].at[pl.ds(0, (RING - 1) * mine)], sem_q, (c, q))]

    q_copies, w_copies, v_copies, p_copies = {}, {}, {}, {}
    for s in streams:
        if s[1] == 0:
            group(cons.at[:, pl.ds(0, (RING - 1) * QUARTERS * ROWS // 2)], sem_init, (s[0],)).wait()
        q_copies[s] = send_grid(s)

    for copy in table_copies:
        copy.wait()
    to_scalar = pltpu.make_async_copy(tables, table_s, sem_local.at[4])
    to_scalar.start()

    def uses(i, h):
        hits = (tables[i] < nb).astype(jnp.float32)
        return hits[2 * h : 2 * h + 1] + hits[2 * h + 1 : 2 * h + 2]

    over = []
    for h in range(2):
        total = uses(0, h)
        for e in range(1, RING):
            total = total + uses((RING - 1) * h + e, h)
        over.append(total)
    partial_v[0] = jnp.where(row == 0, over[0], over[1])
    count_copies = []
    for h, e in near:
        i = (RING - 1) * h + e
        remote(partial_v.at[0], partial_v.at[i], sem_count, (), first(h, e)).start()
    count_copies.append(group(partial_v.at[pl.ds(1, len(near))], sem_count, ()))
    to_scalar.wait()

    def table_of(h, e):
        return 0 if e == 0 else (RING - 1) * h + e

    def live(s):
        return jnp.where(target_ref[0, s] >= 0, 1.0, 0.0).astype(jnp.float32)

    def gather(s, before):
        c, q = s
        h = q % 2
        for copy in q_copies[s]:
            copy.wait_recv()
        for copy in before:
            copy.wait_send()
        grid = bufs["grid", s]
        for e in (1, 3, 2, 0):
            t = table_of(h, 0 if e == 0 else RING - e)

            def one(slot, _):
                value = grid[table_s[t, 4 + h, slot]]
                if e:
                    bufs["back", s][e - 1, slot] = value
                else:
                    bufs["fetched", s][0, slot] = value
                return 0

            lax.fori_loop(0, nb, one, 0, unroll=4)

    def back_send(s):
        c, q = s
        h = q % 2
        for e in (1, 3, 2):
            copy = remote(
                bufs["back", s].at[e - 1], bufs["fetched", s].at[e], sem_w, (c, q), first(h, e)
            )
            copy.start()
        return [group(bufs["back", s], sem_w, (c, q))]

    def update(c, q, step):
        cols = pl.ds(c * LANES, LANES)

        def one(slot, total):
            alive = live(slot)
            for p in range(0, RING, 2):
                value = jnp.concatenate(
                    [bufs["fetched", (c, q)][lax.rem(c1[q % 2] - p - i + RING, RING), slot] for i in range(2)]
                )
                lo = (q * RING + p) * ROWS
                in_block = pl.ds(lo, 2 * ROWS)
                old = dual[slot, in_block, cols]
                at = pl.ds(pl.multiple_of(slot * BLOCK + lo, 2 * ROWS), 2 * ROWS)
                if step > 0:
                    gap = state[at, cols] - value
                    if step < ITERS:
                        total = total + alive * (gap * gap)
                    old = old + alive * gap
                    dual[slot, in_block, cols] = old
                if step < ITERS:
                    drive[at, cols] = (penalty * alive * (value - old)).astype(jnp.bfloat16)
            return total

        total = lax.fori_loop(0, nb, one, jnp.zeros((2 * ROWS, LANES), jnp.float32), unroll=4)
        return total[:ROWS] + total[ROWS:]

    slots_at_once = 4
    chunk = slots_at_once * BLOCK

    def sent(s, e, slots):
        c, q = s
        h = q % 2
        return remote(
            bufs["send", s].at[ring_add(c1[h], e), slots], bufs["got", s].at[e - 1, slots],
            sem_v, (c, q), first(h, e),
        )

    def couple_send(c, step):
        cols = pl.ds(c * LANES, LANES)
        for q in range(QUARTERS):
            for copy in v_copies.get((c, q), ()):
                copy.wait_send()

        def one(i, total):
            at = pl.ds(pl.multiple_of(i * chunk, chunk), chunk)
            rows = base[at, cols] + jnp.dot(
                kkt[at, 0:bound], drive[:, cols], preferred_element_type=jnp.float32
            )
            state[at, cols] = rows
            for j in range(slots_at_once):
                slot = i * slots_at_once + j
                v = rows[j * BLOCK : (j + 1) * BLOCK] + dual[slot, :, cols]
                for q in range(QUARTERS):
                    for p in range(RING):
                        lo = (q * RING + p) * ROWS
                        bufs["send", (c, q)][p, slot] = v[lo : lo + ROWS]
                        if step == ITERS - 1:
                            before = bufs["fetched", (c, q)][lax.rem(c1[q % 2] - p + RING, RING), slot]
                            drift = rows[j * BLOCK + lo : j * BLOCK + lo + ROWS] - before
                            total = total + live(slot) * (drift * drift)
            for q in range(QUARTERS):
                for e in (1, 3, 2):
                    sent((c, q), e, pl.ds(i * slots_at_once, slots_at_once)).start()
            return total

        total = lax.fori_loop(0, nb // slots_at_once, one, zero)
        for q in range(QUARTERS):
            v_copies[c, q] = [group(bufs["got", (c, q)].at[:, pl.ds(0, nb)], sem_v, (c, q))]
        return total

    def reduce_send(s):
        c, q = s
        h = q % 2
        for copy in v_copies[s]:
            copy.wait_recv()
        for copy in p_copies.get(s, ()):
            copy.wait_send()
        mine_at = c1[h]

        def one(pos, _):
            t = table_of(h, 0)
            value = bufs["send", s][mine_at, table_s[t, 2 * h, pos]] + bufs["send", s][mine_at, table_s[t, 2 * h + 1, pos]]
            for e in range(1, RING):
                t = table_of(h, e)
                value = value + bufs["got", s][e - 1, table_s[t, 2 * h, pos]]
                value = value + bufs["got", s][e - 1, table_s[t, 2 * h + 1, pos]]
            bufs["psum", s][pos] = value
            return 0

        lax.fori_loop(0, n_pos, one, 0, unroll=8)
        for e in (1, 3, 2):
            p = ring_add(c2[h], e)
            copy = remote(
                bufs["psum", s].at[pl.ds(pl.multiple_of(p * mine, mine), mine)], bufs["got2", s].at[e - 1],
                sem_p, (c, q), second(h, e),
            )
            copy.start()
        p_copies[s] = [group(bufs["got2", s], sem_p, (c, q))]

    def renew_send(s, moved):
        c, q = s
        h = q % 2
        for copy in p_copies[s]:
            copy.wait_recv()
        for copy in q_copies[s]:
            copy.wait_send()
        for k in range(mine):
            at = c2[h] * mine + k
            total = bufs["psum", s][at]
            for e in range(1, RING):
                total = total + bufs["got2", s][e - 1, k]
            count = count_s[h, at]
            new = total / jnp.maximum(count, 1.0)
            change = new - bufs["grid", s][at]
            moved = moved + count * (change * change)
            bufs["grid", s][at] = new
        q_copies[s] = send_grid(s)
        return moved

    for s in streams:
        gather(s, ())
        w_copies[s] = back_send(s)
    local[2].wait()
    local[4].wait()

    half = 256

    def base_rows(i, _):
        at = pl.ds(pl.multiple_of(i * half, half), half)
        base[at] = jnp.dot(kkt[at], cost[...], preferred_element_type=jnp.float32)
        return 0

    lax.fori_loop(0, kkt.shape[0] // half, base_rows, 0)
    local[3].wait()

    for copy in count_copies:
        copy.wait()
    count_a = partial_v[0, 0:1] + partial_v[RING, 0:1]
    count_b = partial_v[0, 1:2] + partial_v[1, 1:2]
    for e in range(2, RING):
        count_a = count_a + partial_v[RING - 1 + e, 0:1]
        count_b = count_b + partial_v[e, 1:2]
    count_v[...] = jnp.where(row == 0, count_a, count_b)
    counting = pltpu.make_async_copy(count_v, count_s, sem_local.at[5])
    counting.start()
    counting.wait()

    primal = [zero] * ITERS
    moved = [zero] * ITERS
    for step in range(ITERS):
        last = step == ITERS - 1
        for c in range(2):
            for q in range(QUARTERS):
                for copy in w_copies[c, q]:
                    copy.wait_recv()
                got = update(c, q, step)
                if step > 0:
                    primal[step - 1] = primal[step - 1] + got
            primal[step] = primal[step] + couple_send(c, step)
        if last:
            tail = pl.ds(bound, kkt.shape[0] - bound)
            state[tail] = base[tail] + jnp.dot(
                kkt[tail, 0:bound], drive[...], preferred_element_type=jnp.float32
            )
        for s in streams:
            reduce_send(s)
        for s in streams:
            moved[step] = renew_send(s, moved[step])
            if last:
                c, q = s
                h = q % 2
                for e in range(1, RING):
                    p = ring_add(c1[h], e)
                    at = pl.multiple_of(c2[h] * mine + p * owned, owned)
                    copy = remote(
                        bufs["grid", s].at[pl.ds(at, owned)],
                        cons.at[:, shard_rows(q, c1[h]), pl.ds(c * LANES, LANES)],
                        sem_o, (), first(h, e),
                    )
                    copy.start()
                for o in range(owned):
                    at = c2[h] * mine + c1[h] * owned + o
                    cons[o, shard_rows(q, c1[h]), c * LANES : (c + 1) * LANES] = bufs["grid", s][at]
        if not last:
            for s in streams:
                gather(s, w_copies[s])
                w_copies[s] = back_send(s)

    tile = jnp.zeros((8, LANES), jnp.float32)
    for step in range(ITERS):
        tile = jnp.where(row == 2 * step, jnp.sum(primal[step], axis=0, keepdims=True), tile)
        tile = jnp.where(row == 2 * step + 1, jnp.sum(moved[step], axis=0, keepdims=True), tile)
    totals_b[pl.ds(sub, 1)] = tile[None]
    for e in range(1, n_sub):
        pltpu.make_async_remote_copy(
            src_ref=totals_b.at[sub], dst_ref=totals_b.at[sub],
            send_sem=sem_n.at[0, 1], recv_sem=sem_n.at[1, 1],
            device_id={"sub": lax.rem(sub + e, n_sub)}, device_id_type=MESH,
        ).start()
    for s in streams:
        if s == (1, 0):
            group(totals_b.at[pl.ds(0, n_sub - 1)], sem_n, (1,)).wait()
            totals_a[pl.ds(r, 1)] = jnp.sum(totals_b[...], axis=0, keepdims=True)
            for e in range(1, n_region):
                remote(totals_a.at[r], totals_a.at[r], sem_n, (0,), lax.rem(r + e, n_region)).start()
        gather(s, w_copies[s])
        w_copies[s] = back_send(s)

    group(cons.at[:, pl.ds(0, (RING - 1) * QUARTERS * ROWS)], sem_o, ()).wait()
    consensus[...] = cons[...]
    for c in range(2):
        for q in range(QUARTERS):
            for copy in w_copies[c, q]:
                copy.wait_recv()
            update(c, q, ITERS)
    group(totals_a.at[pl.ds(0, n_region - 1)], sem_n, (0,)).wait()
    table = jnp.sum(jnp.sum(totals_a[...], axis=0), axis=1, keepdims=True)
    scale = 1.0 / (n_region * n_sub * 2 * LANES * BLOCK)
    final = 2 * (ITERS - 1)
    rest = table[final : final + 1] - table[final + 1 : final + 2]
    rank = lax.broadcasted_iota(jnp.int32, table.shape, 0)
    table = jnp.where(rank == final, jnp.maximum(rest, 0.0), table)
    table = jnp.where(lax.rem(rank, 2) == 1, (penalty * penalty) * table, table)
    table = jnp.sqrt(table * scale)
    small = (ITERS, 2)
    which = lax.broadcasted_iota(jnp.int32, small, 0) * 2 + lax.broadcasted_iota(jnp.int32, small, 1)
    norms = jnp.zeros(small, jnp.float32)
    for q in range(2 * ITERS):
        norms = jnp.where(which == q, jnp.broadcast_to(table[q : q + 1], small), norms)
    norms_ref[...] = norms

    for s in streams:
        for copy in v_copies[s] + p_copies[s] + q_copies[s] + w_copies[s]:
            copy.wait_send()


def put_out(*refs):
    *arrays, sems = refs
    count = len(arrays) // 2
    copies = [pltpu.make_async_copy(arrays[i], arrays[count + i], sems.at[i]) for i in range(count)]
    for copy in copies:
        copy.start()
    for copy in copies:
        copy.wait()


def shards(kkt_inverse, cost_terms, dual_start, consensus_start, block_target):
    order, scen = cost_terms.shape
    nb = block_target.shape[1]
    owned = consensus_start.shape[0] // BLOCK
    n_region = RING * RING
    n_sub = lax.axis_size("sub")
    n_pos = n_region * owned
    mine = RING * owned
    f32 = jnp.float32
    dma = pltpu.SemaphoreType.DMA
    per_stream = [
        pltpu.VMEM((RING, nb + 1, ROWS, LANES), f32),
        pltpu.VMEM((RING - 1, nb + 1, ROWS, LANES), f32),
        pltpu.VMEM((n_pos, ROWS, LANES), f32),
        pltpu.VMEM((RING - 1, mine, ROWS, LANES), f32),
        pltpu.VMEM((n_pos + 1, ROWS, LANES), f32),
        pltpu.VMEM((RING - 1, nb, ROWS, LANES), f32),
        pltpu.VMEM((RING, nb, ROWS, LANES), f32),
    ]
    state, duals, consensus, norms = pl.pallas_call(
        kernel,
        out_shape=(
            pltpu.VMEM((order, scen), f32),
            pltpu.VMEM((nb, BLOCK, scen), f32),
            pltpu.VMEM((owned, BLOCK, scen), f32),
            pltpu.VMEM((ITERS, 2), f32),
        ),
        in_specs=[pl.BlockSpec(memory_space=pltpu.HBM)] * 5,
        out_specs=(pl.BlockSpec(memory_space=pltpu.VMEM),) * 4,
        scratch_shapes=[
            pltpu.SMEM((1, nb), jnp.int32),
            pltpu.VMEM((order, order), jnp.bfloat16),
            pltpu.VMEM((order, scen), jnp.bfloat16),
            pltpu.VMEM((order, scen), f32),
            pltpu.VMEM((owned, BLOCK, scen), f32),
            pltpu.VMEM((nb * BLOCK, scen), jnp.bfloat16),
            pltpu.VMEM((2 * RING - 1, 8, LANES), jnp.int32),
            pltpu.SMEM((2 * RING - 1, 8, LANES), jnp.int32),
            pltpu.VMEM((2 * RING - 1, 8, LANES), f32),
            pltpu.VMEM((8, LANES), f32),
            pltpu.SMEM((8, LANES), f32),
            pltpu.VMEM((n_region, 8, LANES), f32),
            pltpu.VMEM((n_sub, 8, LANES), f32),
        ]
        + per_stream * (2 * QUARTERS)
        + [
            dma((7,)),
            dma((2,)),
            dma((2,)),
            dma((2, 2)),
            dma((2, 2, QUARTERS)),
            dma((2, 2, QUARTERS)),
            dma((2, 2, QUARTERS)),
            dma((2, 2, QUARTERS)),
            dma((2,)),
            dma((2, 2)),
        ],
        compiler_params=pltpu.CompilerParams(
            collective_id=0, has_side_effects=True, vmem_limit_bytes=40 * 2**20
        ),
        name="admm",
    )(
        *(
            pltpu.with_memory_space_constraint(a, pltpu.HBM)
            for a in (
                kkt_inverse,
                cost_terms,
                dual_start.reshape(nb, BLOCK, scen),
                consensus_start.reshape(owned, BLOCK, scen),
                block_target,
            )
        )
    )
    results = (
        state,
        duals.reshape(nb * BLOCK, scen),
        consensus.reshape(owned * BLOCK, scen),
        norms,
    )
    return pl.pallas_call(
        put_out,
        out_shape=tuple(jax.ShapeDtypeStruct(a.shape, a.dtype) for a in results),
        in_specs=[pl.BlockSpec(memory_space=pltpu.VMEM)] * len(results),
        out_specs=(pl.BlockSpec(memory_space=pl.ANY),) * len(results),
        scratch_shapes=[dma((len(results),))],
        name="put_out",
        compiler_params=pltpu.CompilerParams(vmem_limit_bytes=8 * 2**20),
    )(*(pltpu.with_memory_space_constraint(a, pltpu.VMEM) for a in results))


def solution(mesh):
    both = P(("region", "sub"), None)
    return jax.shard_map(
        shards, mesh=mesh, in_specs=(both,) * 5, out_specs=(both, both, both, P()), check_vma=False
    )
```

```python
import functools

import jax
import jax.numpy as jnp
from jax import lax
from jax.experimental import pallas as pl
from jax.experimental.pallas import tpu as pltpu
from jax.sharding import PartitionSpec as P

MESH = pl.DeviceIdType.MESH
BLOCK = 128
ITERS = 2
RING = 4
QUARTERS = 4
ROWS = 8
LANES = 128
penalty = 1.5


def ring_add(a, e):
    return lax.rem(a + e, RING)


def kernel(
    kkt_ref, cost_ref, dual_ref, cons_ref, target_hbm,
    state, dual, consensus, norms_ref,
    target_ref, kkt, cost, base, cons, drive, tables, table_s, partial_v, count_v, count_s, totals_a, totals_b,
    *rest,
):
    nb = target_hbm.shape[1]
    owned = cons_ref.shape[0]
    n_region = RING * RING
    n_sub = lax.axis_size("sub")
    n_pos = n_region * owned
    mine = RING * owned
    bound = nb * BLOCK
    streams = [(c, q) for c in range(2) for q in range(QUARTERS)]
    bufs = {}
    names = ("send", "got", "psum", "got2", "grid", "back", "fetched")
    rest = list(rest)
    for s in streams:
        for name in names:
            bufs[name, s] = rest.pop(0)
    sem_local, sem_table, sem_count, sem_init, sem_v, sem_p, sem_q, sem_w, sem_o, sem_n = rest

    r = lax.axis_index("region")
    sub = lax.axis_index("sub")
    x = r // RING
    z = lax.rem(r, RING)

    def first(h, e):
        return ring_add(x, e) * RING + z if h == 0 else x * RING + ring_add(z, e)

    def second(h, e):
        return first(1 - h, e)

    c1 = (x, z)
    c2 = (z, x)

    def remote(src, dst, sems, index, region):
        return pltpu.make_async_remote_copy(
            src_ref=src, dst_ref=dst, send_sem=sems.at[(0, *index)], recv_sem=sems.at[(1, *index)],
            device_id={"region": region}, device_id_type=MESH,
        )

    def group(ref, sems, index):
        return remote(ref, ref, sems, index, r)

    local = [
        pltpu.make_async_copy(target_hbm, target_ref, sem_local.at[6]),
        pltpu.make_async_copy(cons_ref, cons, sem_local.at[0]),
        pltpu.make_async_copy(cost_ref, cost, sem_local.at[1]),
        pltpu.make_async_copy(dual_ref, dual, sem_local.at[2]),
        pltpu.make_async_copy(kkt_ref, kkt, sem_local.at[3]),
    ]
    for copy in local[:2]:
        copy.start()

    barrier = pltpu.get_barrier_semaphore()
    near = [(h, e) for h in range(2) for e in range(1, RING)]
    for h, e in near:
        pl.semaphore_signal(barrier, inc=1, device_id={"region": first(h, e)}, device_id_type=MESH)
    for e in range(1, n_sub):
        pl.semaphore_signal(barrier, inc=1, device_id={"sub": lax.rem(sub + e, n_sub)}, device_id_type=MESH)

    local[0].wait()
    lane = lax.broadcasted_iota(jnp.int32, (8, LANES), 1)
    row = lax.broadcasted_iota(jnp.int32, (8, LANES), 0)
    none = jnp.full((8, LANES), nb, jnp.int32)
    one_a, one_b, two_a, two_b = none, none, none, none
    places = jnp.full((8, LANES), n_pos, jnp.int32)
    for s in range(nb):
        t = target_ref[0, s]
        pos_b = t
        pos_a = lax.rem(t // owned, RING) * mine + (t // (owned * RING)) * owned + lax.rem(t, owned)
        pos_a = jnp.where(t >= 0, pos_a, -1)
        hit_a = lane == pos_a
        hit_b = lane == pos_b
        two_a = jnp.where(hit_a & (one_a < nb), s, two_a)
        one_a = jnp.where(hit_a & (one_a == nb), s, one_a)
        two_b = jnp.where(hit_b & (one_b < nb), s, two_b)
        one_b = jnp.where(hit_b & (one_b == nb), s, one_b)
        here = jnp.where(row == 4, pos_a, pos_b)
        places = jnp.where((lane == s) & (t >= 0), here, places)
    tile = jnp.where(row == 0, one_a, places)
    tile = jnp.where(row == 1, two_a, tile)
    tile = jnp.where(row == 2, one_b, tile)
    tile = jnp.where(row == 3, two_b, tile)
    tables[0] = tile

    zero = jnp.zeros((ROWS, LANES), jnp.float32)
    for s in streams:
        for p in range(RING):
            bufs["send", s][p, nb] = zero
        for p in range(RING - 1):
            bufs["got", s][p, nb] = zero
        bufs["grid", s][n_pos] = zero

    local[1].wait()
    pl.semaphore_wait(barrier, len(near) + n_sub - 1)

    def shard_rows(q, p):
        return pl.ds(pl.multiple_of((q * RING + p) * ROWS, ROWS), ROWS)

    for s in streams:
        c, q = s
        h = q % 2
        for e in range(1, RING):
            p = ring_add(c1[h], e)
            at = pl.multiple_of(c2[h] * mine + c1[h] * owned, owned)
            src = cons.at[:, shard_rows(q, p), pl.ds(c * LANES, LANES)]
            remote(src, bufs["grid", s].at[pl.ds(at, owned)], sem_init, (c,), first(h, e)).start()
    table_copies = []
    for h, e in near:
        i = (RING - 1) * h + e
        remote(tables.at[0], tables.at[i], sem_table, (), first(h, e)).start()
    table_copies.append(group(tables.at[pl.ds(1, len(near))], sem_table, ()))
    for copy in local[2:]:
        copy.start()
    for s in streams:
        c, q = s
        h = q % 2
        for o in range(owned):
            at = c2[h] * mine + c1[h] * owned + o
            bufs["grid", s][at] = cons[o, shard_rows(q, c1[h]), c * LANES : (c + 1) * LANES]

    def send_grid(s):
        c, q = s
        h = q % 2
        at = pl.ds(pl.multiple_of(c2[h] * mine, mine), mine)
        for e in range(1, RING):
            copy = remote(
                bufs["grid", s].at[at], bufs["grid", s].at[at], sem_q, (c, q), second(h, e)
            )
            copy.start()
        return [group(bufs["grid", s].at[pl.ds(0, (RING - 1) * mine)], sem_q, (c, q))]

    q_copies, w_copies, v_copies, p_copies = {}, {}, {}, {}
    for s in streams:
        if s[1] == 0:
            group(cons.at[:, pl.ds(0, (RING - 1) * QUARTERS * ROWS // 2)], sem_init, (s[0],)).wait()
        q_copies[s] = send_grid(s)

    for copy in table_copies:
        copy.wait()
    to_scalar = pltpu.make_async_copy(tables, table_s, sem_local.at[4])
    to_scalar.start()

    def uses(i, h):
        hits = (tables[i] < nb).astype(jnp.float32)
        return hits[2 * h : 2 * h + 1] + hits[2 * h + 1 : 2 * h + 2]

    over = []
    for h in range(2):
        total = uses(0, h)
        for e in range(1, RING):
            total = total + uses((RING - 1) * h + e, h)
        over.append(total)
    partial_v[0] = jnp.where(row == 0, over[0], over[1])
    count_copies = []
    for h, e in near:
        i = (RING - 1) * h + e
        remote(partial_v.at[0], partial_v.at[i], sem_count, (), first(h, e)).start()
    count_copies.append(group(partial_v.at[pl.ds(1, len(near))], sem_count, ()))
    to_scalar.wait()

    def table_of(h, e):
        return 0 if e == 0 else (RING - 1) * h + e

    def live(s):
        return jnp.where(target_ref[0, s] >= 0, 1.0, 0.0).astype(jnp.float32)

    def gather(s, before):
        c, q = s
        h = q % 2
        for copy in q_copies[s]:
            copy.wait_recv()
        for copy in before:
            copy.wait_send()
        grid = bufs["grid", s]
        for e in (1, 3, 2, 0):
            t = table_of(h, 0 if e == 0 else RING - e)

            def one(slot, _):
                value = grid[table_s[t, 4 + h, slot]]
                if e:
                    bufs["back", s][e - 1, slot] = value
                else:
                    bufs["fetched", s][0, slot] = value
                return 0

            lax.fori_loop(0, nb, one, 0, unroll=4)

    def back_send(s):
        c, q = s
        h = q % 2
        for e in (1, 3, 2):
            copy = remote(
                bufs["back", s].at[e - 1], bufs["fetched", s].at[e], sem_w, (c, q), first(h, e)
            )
            copy.start()
        return [group(bufs["back", s], sem_w, (c, q))]

    def update(c, q, step):
        cols = pl.ds(c * LANES, LANES)

        def one(slot, total):
            alive = live(slot)
            for p in range(0, RING, 2):
                value = jnp.concatenate(
                    [bufs["fetched", (c, q)][lax.rem(c1[q % 2] - p - i + RING, RING), slot] for i in range(2)]
                )
                lo = (q * RING + p) * ROWS
                in_block = pl.ds(lo, 2 * ROWS)
                old = dual[slot, in_block, cols]
                at = pl.ds(pl.multiple_of(slot * BLOCK + lo, 2 * ROWS), 2 * ROWS)
                if step > 0:
                    gap = state[at, cols] - value
                    if step < ITERS:
                        total = total + alive * (gap * gap)
                    old = old + alive * gap
                    dual[slot, in_block, cols] = old
                if step < ITERS:
                    drive[at, cols] = (penalty * alive * (value - old)).astype(jnp.bfloat16)
            return total

        total = lax.fori_loop(0, nb, one, jnp.zeros((2 * ROWS, LANES), jnp.float32), unroll=4)
        return total[:ROWS] + total[ROWS:]

    slots_at_once = 4
    chunk = slots_at_once * BLOCK

    def sent(s, e, slots):
        c, q = s
        h = q % 2
        return remote(
            bufs["send", s].at[ring_add(c1[h], e), slots], bufs["got", s].at[e - 1, slots],
            sem_v, (c, q), first(h, e),
        )

    def couple_send(c, step):
        cols = pl.ds(c * LANES, LANES)
        for q in range(QUARTERS):
            for copy in v_copies.get((c, q), ()):
                copy.wait_send()

        def one(i, total):
            at = pl.ds(pl.multiple_of(i * chunk, chunk), chunk)
            rows = base[at, cols] + jnp.dot(
                kkt[at, 0:bound], drive[:, cols], preferred_element_type=jnp.float32
            )
            state[at, cols] = rows
            for j in range(slots_at_once):
                slot = i * slots_at_once + j
                v = rows[j * BLOCK : (j + 1) * BLOCK] + dual[slot, :, cols]
                for q in range(QUARTERS):
                    for p in range(RING):
                        lo = (q * RING + p) * ROWS
                        bufs["send", (c, q)][p, slot] = v[lo : lo + ROWS]
                        if step == ITERS - 1:
                            before = bufs["fetched", (c, q)][lax.rem(c1[q % 2] - p + RING, RING), slot]
                            drift = rows[j * BLOCK + lo : j * BLOCK + lo + ROWS] - before
                            total = total + live(slot) * (drift * drift)
            for q in range(QUARTERS):
                for e in (1, 3, 2):
                    sent((c, q), e, pl.ds(i * slots_at_once, slots_at_once)).start()
            return total

        total = lax.fori_loop(0, nb // slots_at_once, one, zero)
        for q in range(QUARTERS):
            v_copies[c, q] = [group(bufs["got", (c, q)].at[:, pl.ds(0, nb)], sem_v, (c, q))]
        return total

    def reduce_send(s):
        c, q = s
        h = q % 2
        for copy in v_copies[s]:
            copy.wait_recv()
        for copy in p_copies.get(s, ()):
            copy.wait_send()
        mine_at = c1[h]

        def one(pos, _):
            t = table_of(h, 0)
            value = bufs["send", s][mine_at, table_s[t, 2 * h, pos]] + bufs["send", s][mine_at, table_s[t, 2 * h + 1, pos]]
            for e in range(1, RING):
                t = table_of(h, e)
                value = value + bufs["got", s][e - 1, table_s[t, 2 * h, pos]]
                value = value + bufs["got", s][e - 1, table_s[t, 2 * h + 1, pos]]
            bufs["psum", s][pos] = value
            return 0

        lax.fori_loop(0, n_pos, one, 0, unroll=8)
        for e in (1, 3, 2):
            p = ring_add(c2[h], e)
            copy = remote(
                bufs["psum", s].at[pl.ds(pl.multiple_of(p * mine, mine), mine)], bufs["got2", s].at[e - 1],
                sem_p, (c, q), second(h, e),
            )
            copy.start()
        p_copies[s] = [group(bufs["got2", s], sem_p, (c, q))]

    def renew_send(s, moved):
        c, q = s
        h = q % 2
        for copy in p_copies[s]:
            copy.wait_recv()
        for copy in q_copies[s]:
            copy.wait_send()
        for k in range(mine):
            at = c2[h] * mine + k
            total = bufs["psum", s][at]
            for e in range(1, RING):
                total = total + bufs["got2", s][e - 1, k]
            count = count_s[h, at]
            new = total / jnp.maximum(count, 1.0)
            change = new - bufs["grid", s][at]
            moved = moved + count * (change * change)
            bufs["grid", s][at] = new
        q_copies[s] = send_grid(s)
        return moved

    for s in streams:
        gather(s, ())
        w_copies[s] = back_send(s)
    local[2].wait()
    local[4].wait()

    half = 256

    def base_rows(i, _):
        at = pl.ds(pl.multiple_of(i * half, half), half)
        base[at] = jnp.dot(kkt[at], cost[...], preferred_element_type=jnp.float32)
        return 0

    lax.fori_loop(0, kkt.shape[0] // half, base_rows, 0)
    local[3].wait()

    for copy in count_copies:
        copy.wait()
    count_a = partial_v[0, 0:1] + partial_v[RING, 0:1]
    count_b = partial_v[0, 1:2] + partial_v[1, 1:2]
    for e in range(2, RING):
        count_a = count_a + partial_v[RING - 1 + e, 0:1]
        count_b = count_b + partial_v[e, 1:2]
    count_v[...] = jnp.where(row == 0, count_a, count_b)
    counting = pltpu.make_async_copy(count_v, count_s, sem_local.at[5])
    counting.start()
    counting.wait()

    primal = [zero] * ITERS
    moved = [zero] * ITERS
    for step in range(ITERS):
        last = step == ITERS - 1
        for c in range(2):
            for q in range(QUARTERS):
                for copy in w_copies[c, q]:
                    copy.wait_recv()
                got = update(c, q, step)
                if step > 0:
                    primal[step - 1] = primal[step - 1] + got
            primal[step] = primal[step] + couple_send(c, step)
        if last:
            tail = pl.ds(bound, kkt.shape[0] - bound)
            state[tail] = base[tail] + jnp.dot(
                kkt[tail, 0:bound], drive[...], preferred_element_type=jnp.float32
            )
        for s in streams:
            reduce_send(s)
        for s in streams:
            moved[step] = renew_send(s, moved[step])
            if last:
                c, q = s
                h = q % 2
                for o in range(owned):
                    at = c2[h] * mine + c1[h] * owned + o
                    cons[o, shard_rows(q, c1[h]), c * LANES : (c + 1) * LANES] = bufs["grid", s][at]
        if not last:
            for s in streams:
                gather(s, w_copies[s])
                w_copies[s] = back_send(s)

    tile = jnp.zeros((8, LANES), jnp.float32)
    for step in range(ITERS):
        tile = jnp.where(row == 2 * step, jnp.sum(primal[step], axis=0, keepdims=True), tile)
        tile = jnp.where(row == 2 * step + 1, jnp.sum(moved[step], axis=0, keepdims=True), tile)
    totals_b[pl.ds(sub, 1)] = tile[None]
    for e in range(1, n_sub):
        pltpu.make_async_remote_copy(
            src_ref=totals_b.at[sub], dst_ref=totals_b.at[sub],
            send_sem=sem_n.at[0, 1], recv_sem=sem_n.at[1, 1],
            device_id={"sub": lax.rem(sub + e, n_sub)}, device_id_type=MESH,
        ).start()
    for s in streams:
        if s == (1, 0):
            group(totals_b.at[pl.ds(0, n_sub - 1)], sem_n, (1,)).wait()
            totals_a[pl.ds(r, 1)] = jnp.sum(totals_b[...], axis=0, keepdims=True)
            for e in range(1, n_region):
                remote(totals_a.at[r], totals_a.at[r], sem_n, (0,), lax.rem(r + e, n_region)).start()
        gather(s, w_copies[s])
        w_copies[s] = back_send(s)

    for s in streams:
        c, q = s
        h = q % 2
        for e in range(1, RING):
            p = ring_add(c1[h], e)
            at = pl.multiple_of(c2[h] * mine + p * owned, owned)
            copy = remote(
                bufs["grid", s].at[pl.ds(at, owned)],
                cons.at[:, shard_rows(q, c1[h]), pl.ds(c * LANES, LANES)],
                sem_o, (), first(h, e),
            )
            copy.start()
    for c in range(2):
        for q in range(QUARTERS):
            for copy in w_copies[c, q]:
                copy.wait_recv()
            update(c, q, ITERS)
    group(cons.at[:, pl.ds(0, (RING - 1) * QUARTERS * ROWS)], sem_o, ()).wait()
    consensus[...] = cons[...]
    group(totals_a.at[pl.ds(0, n_region - 1)], sem_n, (0,)).wait()
    table = jnp.sum(jnp.sum(totals_a[...], axis=0), axis=1, keepdims=True)
    scale = 1.0 / (n_region * n_sub * 2 * LANES * BLOCK)
    final = 2 * (ITERS - 1)
    rest = table[final : final + 1] - table[final + 1 : final + 2]
    rank = lax.broadcasted_iota(jnp.int32, table.shape, 0)
    table = jnp.where(rank == final, jnp.maximum(rest, 0.0), table)
    table = jnp.where(lax.rem(rank, 2) == 1, (penalty * penalty) * table, table)
    table = jnp.sqrt(table * scale)
    small = (ITERS, 2)
    which = lax.broadcasted_iota(jnp.int32, small, 0) * 2 + lax.broadcasted_iota(jnp.int32, small, 1)
    norms = jnp.zeros(small, jnp.float32)
    for q in range(2 * ITERS):
        norms = jnp.where(which == q, jnp.broadcast_to(table[q : q + 1], small), norms)
    norms_ref[...] = norms

    for s in streams:
        for copy in v_copies[s] + p_copies[s] + q_copies[s] + w_copies[s]:
            copy.wait_send()


def put_out(*refs):
    *arrays, sems = refs
    count = len(arrays) // 2
    copies = [pltpu.make_async_copy(arrays[i], arrays[count + i], sems.at[i]) for i in range(count)]
    for copy in copies:
        copy.start()
    for copy in copies:
        copy.wait()


def shards(kkt_inverse, cost_terms, dual_start, consensus_start, block_target):
    order, scen = cost_terms.shape
    nb = block_target.shape[1]
    owned = consensus_start.shape[0] // BLOCK
    n_region = RING * RING
    n_sub = lax.axis_size("sub")
    n_pos = n_region * owned
    mine = RING * owned
    f32 = jnp.float32
    dma = pltpu.SemaphoreType.DMA
    per_stream = [
        pltpu.VMEM((RING, nb + 1, ROWS, LANES), f32),
        pltpu.VMEM((RING - 1, nb + 1, ROWS, LANES), f32),
        pltpu.VMEM((n_pos, ROWS, LANES), f32),
        pltpu.VMEM((RING - 1, mine, ROWS, LANES), f32),
        pltpu.VMEM((n_pos + 1, ROWS, LANES), f32),
        pltpu.VMEM((RING - 1, nb, ROWS, LANES), f32),
        pltpu.VMEM((RING, nb, ROWS, LANES), f32),
    ]
    state, duals, consensus, norms = pl.pallas_call(
        kernel,
        out_shape=(
            pltpu.VMEM((order, scen), f32),
            pltpu.VMEM((nb, BLOCK, scen), f32),
            pltpu.VMEM((owned, BLOCK, scen), f32),
            pltpu.VMEM((ITERS, 2), f32),
        ),
        in_specs=[pl.BlockSpec(memory_space=pltpu.HBM)] * 5,
        out_specs=(pl.BlockSpec(memory_space=pltpu.VMEM),) * 4,
        scratch_shapes=[
            pltpu.SMEM((1, nb), jnp.int32),
            pltpu.VMEM((order, order), jnp.bfloat16),
            pltpu.VMEM((order, scen), jnp.bfloat16),
            pltpu.VMEM((order, scen), f32),
            pltpu.VMEM((owned, BLOCK, scen), f32),
            pltpu.VMEM((nb * BLOCK, scen), jnp.bfloat16),
            pltpu.VMEM((2 * RING - 1, 8, LANES), jnp.int32),
            pltpu.SMEM((2 * RING - 1, 8, LANES), jnp.int32),
            pltpu.VMEM((2 * RING - 1, 8, LANES), f32),
            pltpu.VMEM((8, LANES), f32),
            pltpu.SMEM((8, LANES), f32),
            pltpu.VMEM((n_region, 8, LANES), f32),
            pltpu.VMEM((n_sub, 8, LANES), f32),
        ]
        + per_stream * (2 * QUARTERS)
        + [
            dma((7,)),
            dma((2,)),
            dma((2,)),
            dma((2, 2)),
            dma((2, 2, QUARTERS)),
            dma((2, 2, QUARTERS)),
            dma((2, 2, QUARTERS)),
            dma((2, 2, QUARTERS)),
            dma((2,)),
            dma((2, 2)),
        ],
        compiler_params=pltpu.CompilerParams(
            collective_id=0, has_side_effects=True, vmem_limit_bytes=40 * 2**20
        ),
        name="admm",
    )(
        *(
            pltpu.with_memory_space_constraint(a, pltpu.HBM)
            for a in (
                kkt_inverse,
                cost_terms,
                dual_start.reshape(nb, BLOCK, scen),
                consensus_start.reshape(owned, BLOCK, scen),
                block_target,
            )
        )
    )
    results = (
        state,
        duals.reshape(nb * BLOCK, scen),
        consensus.reshape(owned * BLOCK, scen),
        norms,
    )
    return pl.pallas_call(
        put_out,
        out_shape=tuple(jax.ShapeDtypeStruct(a.shape, a.dtype) for a in results),
        in_specs=[pl.BlockSpec(memory_space=pltpu.VMEM)] * len(results),
        out_specs=(pl.BlockSpec(memory_space=pl.ANY),) * len(results),
        scratch_shapes=[dma((len(results),))],
        name="put_out",
        compiler_params=pltpu.CompilerParams(vmem_limit_bytes=8 * 2**20),
    )(*(pltpu.with_memory_space_constraint(a, pltpu.VMEM) for a in results))


def solution(mesh):
    both = P(("region", "sub"), None)
    return jax.shard_map(
        shards, mesh=mesh, in_specs=(both,) * 5, out_specs=(both, both, both, P()), check_vma=False
    )
```
